512 devices in a mesh: chan: 64 (over z, x), tm: 8 (over y, core).
Axes of the slice: x: 4, y: 4, z: 16, core: 2. Of those that a mesh axis runs over, the one named last changes fastest.
Arguments:
- samples: bfloat16 [128, 2097152], P('chan', 'tm'), may hold values from -8 to 8
- taps: float32 [16, 4096], replicated, may hold values from -0.0234375 to 0.0234375
- steering: float32 [8, 128], replicated, may hold values from -6 to 6
- interferer_ids: int32 [2048, 4], P(('chan', 'tm')), may hold values from 0 to 7, all different within a row
- ranks: int32 [2048], P(('chan', 'tm')), may hold values from 0 to 4
Outputs:
- covariance: float32 [2048, 2, 128, 128], P(('chan', 'tm'))
The draws below stay inside these ranges and needn't reach their ends.
Inputs may be any that keep to these rules, and one draw needn't show every extreme that they name: `interferer_ids`: the 4 entries of one channel's row name different directions.
All inputs are finite; a program needn't handle non-finite values.
Results may differ from the reference program's by a relative error of at most 0.00075.
Values may be sent and summed in bfloat16 or wider, within the bound.
A program may use at most 64 MiB of HBM per device.

```python
import jax
import jax.numpy as jnp
from jax import lax

ARRAY_ELEMENTS = 128
KEPT_CHANNELS = 2048
TAPS = 16
JAMMER_BEARINGS = 8
RMAX = 4
L = 4096
FRAMES = 512


def mixing(key):
    sample_values = jax.random.normal(jax.random.fold_in(key, 11), (JAMMER_BEARINGS, ARRAY_ELEMENTS), jnp.float32)
    return jnp.clip(sample_values, -6.0, 6.0)


def draw_steering(key, part):
    return mixing(key)


def draw_samples(key, part):
    overall_length = FRAMES * L
    jitter_key = jax.random.fold_in(key, 23)
    source_key = jax.random.fold_in(key, 29)
    thermal_jitter = jax.random.normal(jitter_key, (ARRAY_ELEMENTS, overall_length), jnp.float32)
    strength = 0.5
    sources = jax.random.normal(source_key, (JAMMER_BEARINGS, overall_length), jnp.float32) * strength
    mixer = mixing(key)
    mixed = thermal_jitter
    for direction in range(JAMMER_BEARINGS):
        mixed = mixed + mixer[direction][:, None] * sources[direction][None, :]
    return jnp.clip(mixed, -8.0, 8.0).astype(jnp.bfloat16)


def place_ends(result, stream_key, smallest, largest):
    longest = result.shape.index(max(result.shape))
    spots = []
    for shift in (0, 1):
        where = [jax.random.randint(jax.random.fold_in(stream_key, axis), (), 0, length) for axis, length in enumerate(result.shape)]
        where[longest] = (where[longest] + shift) % result.shape[longest]
        spots.append(tuple(where))
    return result.at[spots[0]].set(smallest).at[spots[1]].set(largest)


def choose_distinct(key, rows, count, top, lift):
    sequence = jax.random.permutation(jax.random.fold_in(key, 1), count)
    boost = sequence
    for power in range(3):
        boost = boost * boost // count
    boost = boost * lift // count
    chance = jax.random.randint(jax.random.fold_in(key, 2), (rows, count), 0, 4096) + boost
    fixed_rows = jax.random.permutation(jax.random.fold_in(key, 3), rows)[jnp.arange(count) % rows]
    chance = jnp.where(jnp.arange(rows)[:, None] == fixed_rows[None, :], 1 << 14, chance)
    merit = chance * count + jnp.arange(count)
    return lax.top_k(merit.astype(jnp.int32), top)[1].astype(jnp.int32)


def normal_values(rng, dims, spread, limit, held_as=jnp.bfloat16):
    array = spread * jax.random.normal(rng, dims, jnp.float32)
    return jnp.clip(array, min=-limit, max=limit).astype(held_as)


def setup_inputs(seed: int = 0) -> dict:
    splits = jax.random.split(jax.random.key(seed), 6)
    samples = draw_samples(jax.random.fold_in(splits[5], 71), 0)
    taps = normal_values(splits[1], (TAPS, L), (TAPS * L) ** -0.5, 0.0234375, jnp.float32)
    steering = draw_steering(jax.random.fold_in(splits[5], 71), 0)
    interferer_ids = choose_distinct(splits[3], KEPT_CHANNELS, JAMMER_BEARINGS, RMAX, 0)
    ranks = place_ends(jax.random.randint(splits[4], (KEPT_CHANNELS,), 0, RMAX + 1), jax.random.fold_in(splits[4], 1), 0, RMAX).astype(jnp.int32)
    return dict(samples=samples, taps=taps, steering=steering, interferer_ids=interferer_ids, ranks=ranks)


epsilon = 1e-06
highest = lax.Precision.HIGHEST

def orthonormal(vectors):
    found = []
    for column in range(vectors.shape[1]):
        residue = vectors[:, column, :]
        for earlier in found:
            residue = residue - earlier * lax.optimization_barrier(jnp.sum(earlier * residue, axis=-1, keepdims=True))
        found.append(residue / jnp.sqrt(lax.optimization_barrier(jnp.sum(residue * residue, axis=-1, keepdims=True)) + epsilon))
    return jnp.stack(found, axis=1)

def project_out(gram, chosen, counted, steering, frame_total):
    slots = chosen.shape[1]
    live = (jnp.arange(slots, dtype=jnp.int32)[None, :] < counted[:, None]).astype(jnp.float32)
    vectors = steering[chosen] * live[:, :, None]
    basis = orthonormal(vectors)
    left = jnp.einsum('cra,csab->csrb', basis, gram, precision=highest)
    right = jnp.einsum('csab,crb->csar', gram, basis, precision=highest)
    core = jnp.einsum('csrb,ctb->csrt', left, basis, precision=highest)
    inner = jnp.einsum('csrt,ctb->csrb', core, basis, precision=highest)
    suppressed_output = gram - jnp.einsum('cra,csrb->csab', basis, left, precision=highest)
    suppressed_output = suppressed_output - jnp.einsum('csar,crb->csab', right, basis, precision=highest)
    suppressed_output = suppressed_output + jnp.einsum('cra,csrb->csab', basis, inner, precision=highest)
    return suppressed_output / frame_total

def reference(samples, taps, steering, interferer_ids, ranks):

    def channelize(signal):
        blocks = signal.astype(jnp.float32).reshape(FRAMES, L)
        padded = jnp.concatenate([jnp.zeros((TAPS - 1, L), jnp.float32), blocks], axis=0)
        filtered = jnp.zeros((FRAMES, L), jnp.float32)
        for tap_index in range(TAPS):
            filtered = filtered + taps[tap_index] * padded[tap_index:tap_index + FRAMES]
        spectrum = jnp.fft.rfft(filtered, axis=-1)[:, :KEPT_CHANNELS]
        return jnp.stack([jnp.real(spectrum), jnp.imag(spectrum)], axis=0).astype(jnp.bfloat16)
    spectra = lax.map(channelize, samples)
    width = 64

    def per_block(start):
        piece = lax.dynamic_slice_in_dim(spectra, start, width, axis=3).astype(jnp.float32)
        outer = jnp.einsum('arfc,bsfc->crasb', piece, piece, precision=highest)
        real_part = outer[:, 0, :, 0, :] + outer[:, 1, :, 1, :]
        imag_part = outer[:, 1, :, 0, :] - outer[:, 0, :, 1, :]
        gram = jnp.stack([real_part, imag_part], axis=1)
        chosen = lax.dynamic_slice_in_dim(interferer_ids, start, width, axis=0)
        counted = lax.dynamic_slice_in_dim(ranks, start, width, axis=0)
        return project_out(gram, chosen, counted, steering, FRAMES)
    starts = (jnp.arange(KEPT_CHANNELS // width) * width).astype(jnp.int32)
    suppressed_output = lax.map(per_block, starts)
    return suppressed_output.reshape(KEPT_CHANNELS, 2, ARRAY_ELEMENTS, ARRAY_ELEMENTS)
```

```python
import jax
import jax.numpy as jnp
import numpy as np
from jax import lax
from jax.experimental import pallas as pl
from jax.experimental.pallas import tpu as pltpu
from jax.sharding import PartitionSpec as P

SLOW = 32
FAST = 128
EPSILON = 1e-06
F32 = jnp.float32
BF16 = jnp.bfloat16
HIGHEST = lax.Precision.HIGHEST


def split_constant(values):
    high = values.astype(np.float32).astype(jnp.bfloat16)
    low = (values - high.astype(np.float64)).astype(np.float32).astype(jnp.bfloat16)
    return high, low


def first_stage_matrix():
    p = np.arange(SLOW)
    rows = [np.ones(SLOW), (-1.0) ** p]
    for k1 in range(1, SLOW // 2):
        rows.append(np.cos(2.0 * np.pi * (k1 * p % SLOW) / SLOW))
        rows.append(-np.sin(2.0 * np.pi * (k1 * p % SLOW) / SLOW))
    coefficients = np.stack(rows)
    full = np.einsum("kp,fg->kfgp", coefficients, np.eye(8)).reshape(SLOW * 8, 8 * SLOW)
    return split_constant(full)


def second_stage_matrix():
    turns = np.outer(np.arange(64), np.arange(FAST)) % FAST
    angle = 2.0 * np.pi * turns / FAST
    real_rows = np.concatenate([np.cos(angle), np.sin(angle)], axis=1)
    imag_rows = np.concatenate([-np.sin(angle), np.cos(angle)], axis=1)
    high, low = split_constant(np.concatenate([real_rows, imag_rows], axis=0))
    return np.concatenate([high, low], axis=0)


def twiddles():
    angle = 2.0 * np.pi * np.outer(np.arange(SLOW), np.arange(FAST)) / (SLOW * FAST)
    return np.cos(angle).astype(np.float32), np.sin(angle).astype(np.float32)


def split(values):
    high = values.astype(BF16)
    return high, (values - high.astype(F32)).astype(BF16)


def dot(a, b):
    return lax.dot_general(a, b, (((1,), (0,)), ((), ())), preferred_element_type=F32)


def dot_t(a, b):
    return lax.dot_general(a, b, (((1,), (1,)), ((), ())), preferred_element_type=F32)


def channelize_kernel(now_ref, before_ref, taps_ref, w1h_ref, w1l_ref, w2_ref, cos_ref, sin_ref, out_ref,
                      window, filtered, y, spectrum):
    tap_count = taps_ref.shape[0]
    halo = tap_count - 1
    frames = now_ref.shape[0]
    rows = now_ref.shape[1]
    window[0:halo] = before_ref[...].astype(F32)

    def widen(g, carry):
        at = pl.multiple_of(g * 8, 8)
        window[pl.ds(halo + at, 8)] = now_ref[pl.ds(at, 8)].astype(F32)
        return carry

    lax.fori_loop(0, frames // 8, widen, 0)

    def group(g, carry):
        first = pl.multiple_of(g * 8, 8)
        for r in range(0, rows, 8):
            weights = [taps_ref[t, r : r + 8, :] for t in range(tap_count)]
            seen = [window[first + i, r : r + 8, :] for i in range(8 + halo)]
            for f in range(8):
                total = weights[0] * seen[f]
                for t in range(1, tap_count):
                    total = total + weights[t] * seen[f + t]
                filtered[f, r : r + 8, :] = total
        columns_h, columns_l = [], []
        for a in range(2):
            parts = [split(filtered[f, pl.ds(a, SLOW, stride=2), :]) for f in range(8)]
            columns_h.append(jnp.concatenate([h for h, _ in parts], axis=0))
            columns_l.append(jnp.concatenate([l for _, l in parts], axis=0))
        xh = jnp.concatenate(columns_h, axis=1)
        xl = jnp.concatenate(columns_l, axis=1)
        turned = dot(w1h_ref[...], xh) + dot(w1h_ref[...], xl) + dot(w1l_ref[...], xh)
        for a in range(2):
            piece = turned[:, a * FAST : (a + 1) * FAST].reshape(SLOW, 8, FAST)
            y[:, pl.ds(pl.multiple_of(a * frames + g * 8, 8), 8), :] = piece
        return carry

    lax.fori_loop(0, frames // 8, group, 0)

    w2 = w2_ref[...]
    w2h = w2[:FAST]

    def finish(zr, zi, k1):
        zh, zl = split(jnp.concatenate([zr, zi], axis=1))
        both = dot_t(w2, zh)
        result = both[:FAST] + both[FAST:] + dot_t(w2h, zl)
        for part in range(2):
            start = (k1 // 4) * 8 + part * 4 + k1 % 4
            spectrum[pl.ds(start, 64, stride=64), :] = result[part * 64 : (part + 1) * 64]

    for k1 in (0, SLOW // 2):
        real = y[0 if k1 == 0 else 1]
        finish(real * cos_ref[k1 : k1 + 1, :], -real * sin_ref[k1 : k1 + 1, :], k1)
    for k1 in range(1, SLOW // 2):
        real, imag = y[2 * k1], y[2 * k1 + 1]
        c, s = cos_ref[k1 : k1 + 1, :], sin_ref[k1 : k1 + 1, :]
        finish(real * c + imag * s, imag * c - real * s, k1)
        k1 = SLOW - k1
        c, s = cos_ref[k1 : k1 + 1, :], sin_ref[k1 : k1 + 1, :]
        finish(real * c - imag * s, -imag * c - real * s, k1)

    def pack(i, carry):
        at = pl.multiple_of(i * 32, 32)
        out_ref[pl.ds(at, 32)] = spectrum[pl.ds(pl.multiple_of(at * 8, 256), 256), :].reshape(32, 8, FAST).astype(BF16)
        return carry

    lax.fori_loop(0, 16, pack, 0)


def channelize(now, before, taps):
    frames, rows, _ = now.shape
    w1h, w1l = first_stage_matrix()
    cos, sin = twiddles()
    vmem = pl.BlockSpec(memory_space=pltpu.VMEM)
    return pl.pallas_call(
        channelize_kernel,
        out_shape=jax.ShapeDtypeStruct((512, 8, FAST), BF16),
        in_specs=[vmem] * 8,
        out_specs=vmem,
        scratch_shapes=[
            pltpu.VMEM((frames + before.shape[0], rows, FAST), F32),
            pltpu.VMEM((8, rows, FAST), F32),
            pltpu.VMEM((SLOW, 2 * frames, FAST), F32),
            pltpu.VMEM((4096, FAST), F32),
        ],
        compiler_params=pltpu.CompilerParams(vmem_limit_bytes=40 << 20),
        cost_estimate=pl.CostEstimate(flops=10**9, bytes_accessed=4 << 20, transcendentals=0),
    )(now, before, taps, jnp.asarray(w1h), jnp.asarray(w1l), jnp.asarray(second_stage_matrix()),
      jnp.asarray(cos), jnp.asarray(sin))


def exchange_kernel(extents, near, src_ref, dst_ref, send_sem, recv_sem, local_sem, plane_sem, whole_sem):
    nz, nx, ny, nc = extents
    nt = ny * nc
    total = nz * nx * nt
    group = lax.axis_index("chan")
    shard = lax.axis_index("tm")
    z, x = group // nx, lax.rem(group, nx)
    yy, core = shard // nc, lax.rem(shard, nc)
    me = shard * (nz * nx) + group

    def along_z(d):
        return {"chan": lax.rem(z + d, nz) * nx + x}

    def along_x(d):
        return {"chan": z * nx + lax.rem(x + d, nx)}

    def along_t(d):
        return {"tm": lax.rem(shard + d, nt)}

    barrier = pltpu.get_barrier_semaphore()
    for count, line in ((nz, along_z), (nx, along_x), (nt, along_t)):
        for d in range(1, count):
            pl.semaphore_signal(barrier, inc=1, device_id=line(d))
    pl.semaphore_wait(barrier, nz + nx + nt - 3)
    for d in range(1, nz):
        pl.semaphore_signal(plane_sem, inc=1, device_id=along_z(d))
    pl.semaphore_wait(plane_sem, nz - 1)
    for d in range(1, nx):
        pl.semaphore_signal(whole_sem, inc=1, device_id=along_x(d))
    pl.semaphore_wait(whole_sem, nx - 1)

    def send(dz, r):
        dx, dy, dc = lax.rem(r, nx), lax.rem(r // nx, ny), r // (nx * ny)
        to_group = lax.rem(z + dz, nz) * nx + lax.rem(x + dx, nx)
        to_shard = lax.rem(yy + dy, ny) * nc + lax.rem(core + dc, nc)
        pltpu.make_async_remote_copy(
            src_ref=src_ref.at[to_group * nt + to_shard],
            dst_ref=dst_ref.at[me],
            send_sem=send_sem,
            recv_sem=recv_sem,
            device_id={"chan": to_group, "tm": to_shard},
        ).start()

    for dz in near:
        if dz:
            send(dz, jnp.int32(0))

    def rest(r, carry):
        for dz in near:
            send(dz, r)
        return carry

    lax.fori_loop(1, nx * ny * nc, rest, 0)
    own = pltpu.make_async_copy(src_ref.at[group * nt + shard], dst_ref.at[me], local_sem)
    own.start()
    own.wait()
    others = pl.ds(0, total - 1)
    pltpu.make_async_copy(src_ref.at[others], src_ref.at[others], send_sem).wait()
    pltpu.make_async_copy(dst_ref.at[others], dst_ref.at[others], recv_sem).wait()


def exchange(pieces):
    extents = (16, 4, 4, 2)
    near = [8]
    for d in range(1, 8):
        near += [d, 16 - d]
    near.append(0)

    def kernel(*refs):
        exchange_kernel(extents, near, *refs)

    vmem = pl.BlockSpec(memory_space=pltpu.VMEM)
    return pl.pallas_call(
        kernel,
        out_shape=jax.ShapeDtypeStruct(pieces.shape, pieces.dtype),
        in_specs=[vmem],
        out_specs=vmem,
        scratch_shapes=[pltpu.SemaphoreType.DMA] * 3 + [pltpu.SemaphoreType.REGULAR] * 2,
        compiler_params=pltpu.CompilerParams(collective_id=0, has_side_effects=True, vmem_limit_bytes=16 << 20),
    )(pieces)


def orthonormal(vectors):
    found = []
    for column in range(vectors.shape[1]):
        residue = vectors[:, column, :]
        for earlier in found:
            residue = residue - earlier * jnp.sum(earlier * residue, axis=-1, keepdims=True)
        found.append(residue / jnp.sqrt(jnp.sum(residue * residue, axis=-1, keepdims=True) + EPSILON))
    return jnp.stack(found, axis=1)


def projectors(chosen, counted, steering):
    count, slots = chosen.shape
    directions, antennas = steering.shape
    onehot = (chosen[:, :, None] == lax.broadcasted_iota(jnp.int32, (count, slots, directions), 2)).astype(F32)
    live = (lax.broadcasted_iota(jnp.int32, (count, slots), 1) < counted[:, None]).astype(F32)
    vectors = jnp.einsum("crn,na->cra", onehot, steering, precision=HIGHEST) * live[:, :, None]
    basis = orthonormal(vectors)
    return jnp.eye(antennas, dtype=F32) - jnp.einsum("cra,crb->cab", basis, basis, precision=HIGHEST)


def covariance_kernel(frame_total, received_ref, projector_ref, out_ref, wide, rows):
    lane = lax.broadcasted_iota(jnp.int32, (64, FAST), 1)
    lower = lane < 64
    shards = received_ref.shape[0] // 64
    for t in range(shards):
        wide[pl.ds(t * 512, 512), :] = received_ref[pl.ds(t * 64, 64)].astype(F32).reshape(512, FAST)
    for channel in range(4):
        for part in range(2):
            for t in range(0, shards, 2):
                a = wide[pl.ds(t * 512 + part * 4 + channel, 64, stride=8), :]
                b = wide[pl.ds((t + 1) * 512 + part * 4 + channel, 64, stride=8), :]
                first = jnp.where(lower, a, pltpu.roll(b, 64, 1))
                second = jnp.where(lower, pltpu.roll(a, 64, 1), b)
                rows[t // 2, pl.ds(part * 128, 64, stride=2), :] = first
                rows[t // 2, pl.ds(part * 128 + 1, 64, stride=2), :] = second
        x = jnp.concatenate([rows[i].astype(BF16) for i in range(shards // 2)], axis=1)
        outer = dot_t(x, x)
        gram_real = outer[:128, :128] + outer[128:, 128:]
        gram_imag = outer[128:, :128] - outer[:128, 128:]
        keep = projector_ref[channel]
        left = jnp.dot(jnp.concatenate([gram_real, gram_imag], axis=0), keep, precision=HIGHEST, preferred_element_type=F32)
        both = jnp.concatenate([left[:128], left[128:]], axis=1)
        done = jnp.dot(keep, both, precision=HIGHEST, preferred_element_type=F32) * (1.0 / frame_total)
        out_ref[channel, 0] = done[:, :128]
        out_ref[channel, 1] = done[:, 128:]


def covariance(received, keep, frame_total):
    def kernel(*refs):
        covariance_kernel(frame_total, *refs)

    vmem = pl.BlockSpec(memory_space=pltpu.VMEM)
    return pl.pallas_call(
        kernel,
        out_shape=jax.ShapeDtypeStruct((4, 2, 128, 128), F32),
        in_specs=[vmem] * 2,
        out_specs=vmem,
        scratch_shapes=[pltpu.VMEM((4096, FAST), F32), pltpu.VMEM((4, 256, FAST), F32)],
        compiler_params=pltpu.CompilerParams(vmem_limit_bytes=24 << 20),
        cost_estimate=pl.CostEstimate(flops=10**9, bytes_accessed=2 << 20, transcendentals=0),
    )(received, keep)


def per_device(samples, taps, steering, interferer_ids, ranks):
    antennas, width = samples.shape
    tap_count, length = taps.shape
    frames = width // length
    peers = lax.axis_size("tm")
    blocks = samples.reshape(antennas, frames * SLOW, FAST).transpose(1, 0, 2).reshape(frames, SLOW * antennas, FAST)
    before = lax.ppermute(blocks[frames - tap_count + 1 :], "tm", [(i, i + 1) for i in range(peers - 1)])
    weights = jnp.repeat(taps.reshape(tap_count, SLOW, FAST), antennas, axis=1)
    pieces = channelize(blocks, before, weights)
    received = exchange(pieces)
    keep = projectors(interferer_ids, ranks, steering)
    return covariance(received, keep, frames * peers)


def solution(mesh):
    in_specs = (P("chan", "tm"), P(), P(), P(("chan", "tm"), None), P(("chan", "tm")))
    out_specs = P(("chan", "tm"), None, None, None)
    return jax.shard_map(per_device, mesh=mesh, in_specs=in_specs, out_specs=out_specs, check_vma=False)
```

```python
import jax
import jax.numpy as jnp
import numpy as np
from jax import lax
from jax.experimental import pallas as pl
from jax.experimental.pallas import tpu as pltpu
from jax.sharding import PartitionSpec as P

SLOW = 32
FAST = 128
EPSILON = 1e-06
F32 = jnp.float32
BF16 = jnp.bfloat16
HIGHEST = lax.Precision.HIGHEST


def split_constant(values):
    high = values.astype(np.float32).astype(jnp.bfloat16)
    low = (values - high.astype(np.float64)).astype(np.float32).astype(jnp.bfloat16)
    return high, low


def first_stage_matrix():
    p = np.arange(SLOW)
    rows = []
    for k1 in range(SLOW // 2 + 1):
        angle = 2.0 * np.pi * (k1 * p % SLOW) / SLOW
        rows.append(np.cos(angle))
        rows.append(-np.sin(angle) if k1 % (SLOW // 2) else np.zeros(SLOW))
    coefficients = np.stack(rows)
    full = np.einsum("kp,fg->kfgp", coefficients, np.eye(8)).reshape(len(rows) * 8, 8 * SLOW)
    return split_constant(full)


def second_stage_matrix():
    turns = np.outer(np.arange(64), np.arange(FAST)) % FAST
    angle = 2.0 * np.pi * turns / FAST
    real_rows = np.concatenate([np.cos(angle), np.sin(angle)], axis=1)
    imag_rows = np.concatenate([-np.sin(angle), np.cos(angle)], axis=1)
    high, low = split_constant(np.concatenate([real_rows, imag_rows], axis=0))
    return np.concatenate([high, low], axis=0)


def twiddles():
    angle = 2.0 * np.pi * np.outer(np.arange(SLOW), np.arange(FAST)) / (SLOW * FAST)
    sign = np.where(np.arange(SLOW) > SLOW // 2, -1.0, 1.0)[:, None]
    return np.stack([np.cos(angle), np.sin(angle), sign * np.cos(angle), sign * np.sin(angle)]).astype(np.float32)


def split(values):
    high = values.astype(BF16)
    return high, (values - high.astype(F32)).astype(BF16)


def dot(a, b):
    return lax.dot_general(a, b, (((1,), (0,)), ((), ())), preferred_element_type=F32)


def dot_t(a, b):
    return lax.dot_general(a, b, (((1,), (1,)), ((), ())), preferred_element_type=F32)


def spectra_kernel(extents, near, now_ref, taps_ref, w1_ref, w2_ref, table_ref, steering_ref, chosen_ref, counted_ref,
                   dst_ref, basis_ref, arrived, window, weights, filtered, y, spectrum, pieces, w1, w2, table,
                   in_sem, const_sem, halo_send, halo_recv, send_sem, recv_sem, local_sem, plane_sem, whole_sem):
    nz, nx, ny, nc = extents
    nt = ny * nc
    total = nz * nx * nt
    tap_count = taps_ref.shape[0]
    halo = tap_count - 1
    frames, rows, _ = now_ref.shape
    group = lax.axis_index("chan")
    shard = lax.axis_index("tm")
    z, x = group // nx, lax.rem(group, nx)
    me = shard * (nz * nx) + group

    def along_z(d):
        return {"chan": lax.rem(z + d, nz) * nx + x}

    def along_x(d):
        return {"chan": z * nx + lax.rem(x + d, nx)}

    def along_t(d):
        return {"tm": lax.rem(shard + d, nt)}

    constants = [
        pltpu.make_async_copy(source, target, const_sem.at[i])
        for i, (source, target) in enumerate(((w1_ref, w1), (w2_ref, w2), (table_ref, table)))
    ]
    inputs = [
        pltpu.make_async_copy(now_ref.at[pl.ds(i * 16, 16)], arrived.at[pl.ds(halo + i * 16, 16)], in_sem.at[i])
        for i in range(frames // 16)
    ]
    for copy in inputs + constants:
        copy.start()

    barrier = pltpu.get_barrier_semaphore()
    for count, line in ((nt, along_t), (nz, along_z), (nx, along_x)):
        for d in range(1, count):
            pl.semaphore_signal(barrier, inc=1, device_id=line(d))

    for a in range(2):
        for t in range(tap_count):
            weights[t, pl.ds(a, SLOW, stride=2), :] = taps_ref[t]

    @pl.when(shard == 0)
    def _():
        arrived[0:halo] = jnp.zeros((halo, rows, FAST), BF16)

    pl.semaphore_wait(barrier, nz + nx + nt - 3)
    carried = pltpu.make_async_remote_copy(
        src_ref=now_ref.at[pl.ds(frames - halo, halo)],
        dst_ref=arrived.at[pl.ds(0, halo)],
        send_sem=halo_send,
        recv_sem=halo_recv,
        device_id=along_t(1),
    )

    @pl.when(shard < nt - 1)
    def _():
        carried.start()

    for d in range(1, nz):
        pl.semaphore_signal(plane_sem, inc=1, device_id=along_z(d))

    for i, copy in enumerate(inputs):
        copy.wait()

        def widen(g, carry, i=i):
            at = halo + i * 16 + g * 8
            window[pl.ds(at, 8)] = arrived[pl.ds(at, 8)].astype(F32)
            return carry

        lax.fori_loop(0, 2, widen, 0)

    def filter_group(g, carry):
        first = pl.multiple_of(g * 8, 8)
        for r in range(0, rows, 8):
            tap = [weights[t, r : r + 8, :] for t in range(tap_count)]
            seen = [window[first + i, r : r + 8, :] for i in range(8 + halo)]
            for f in range(8):
                result = tap[0] * seen[f]
                for t in range(1, tap_count):
                    result = result + tap[t] * seen[f + t]
                filtered[f, r : r + 8, :] = result
        columns_h, columns_l = [], []
        for a in range(2):
            parts = [split(filtered[f, pl.ds(a, SLOW, stride=2), :]) for f in range(8)]
            columns_h.append(jnp.concatenate([h for h, _ in parts], axis=0))
            columns_l.append(jnp.concatenate([l for _, l in parts], axis=0))
        xh = jnp.concatenate(columns_h, axis=1)
        xl = jnp.concatenate(columns_l, axis=1)
        turned = dot(w1[0], xh) + dot(w1[0], xl) + dot(w1[1], xh)
        for a in range(2):
            piece = turned[:, a * FAST : (a + 1) * FAST].reshape(SLOW + 2, 8, FAST)
            y[:, pl.ds(pl.multiple_of(a * frames + g * 8, 8), 8), :] = piece
        return carry

    constants[0].wait()
    lax.fori_loop(2, 5, filter_group, 0)
    pl.semaphore_wait(plane_sem, nz - 1)
    for d in range(1, nx):
        pl.semaphore_signal(whole_sem, inc=1, device_id=along_x(d))
    lax.fori_loop(5, 8, filter_group, 0)

    @pl.when(shard > 0)
    def _():
        carried.wait_recv()

    @pl.when(shard < nt - 1)
    def _():
        carried.wait_send()

    window[0:halo] = arrived[0:halo].astype(F32)
    lax.fori_loop(0, 2, filter_group, 0)
    pl.semaphore_wait(whole_sem, nx - 1)
    constants[1].wait()
    constants[2].wait()
    own = pltpu.make_async_copy(pieces.at[group], dst_ref.at[me], local_sem)

    def finish(i, carry):
        to_shard = lax.rem(shard + i, nt)
        for sub in range(4):
            k1 = to_shard * 4 + sub
            j = jnp.minimum(k1, SLOW - k1)
            real, imag = y[2 * j], y[2 * j + 1]
            cos, sin, signed_cos, signed_sin = (table[n, pl.ds(k1, 1), :] for n in range(4))
            zr = real * cos + imag * signed_sin
            zi = imag * signed_cos - real * sin
            zh, zl = split(jnp.concatenate([zr, zi], axis=1))
            both = dot_t(w2[...], zh)
            result = both[:FAST] + both[FAST:] + dot_t(w2[:FAST], zl)
            for part in range(2):
                spectrum[pl.ds(part * 4 + sub, 64, stride=8), :] = result[part * 64 : (part + 1) * 64]
        base = pl.multiple_of(i * 64, 64)
        pieces[pl.ds(base, 64)] = spectrum[...].reshape(64, 8, FAST).astype(BF16)

        def send(dz, dx):
            to_group = lax.rem(z + dz, nz) * nx + lax.rem(x + dx, nx)
            pltpu.make_async_remote_copy(
                src_ref=pieces.at[base + to_group],
                dst_ref=dst_ref.at[me],
                send_sem=send_sem,
                recv_sem=recv_sem,
                device_id={"chan": to_group, "tm": to_shard},
            ).start()

        def column(dx, inner):
            for dz in near:
                if dz:
                    send(dz, dx)
                else:

                    @pl.when(i + dx > 0)
                    def _():
                        send(0, dx)

            return inner

        lax.fori_loop(0, nx, column, 0)
        return carry

    lax.fori_loop(0, nt, finish, 0)
    own.start()

    found = []
    for slot in range(chosen_ref.shape[1]):
        wanted = chosen_ref[:, slot : slot + 1]
        residue = jnp.zeros((chosen_ref.shape[0], FAST), F32)
        for direction in range(steering_ref.shape[0]):
            residue = jnp.where(wanted == direction, steering_ref[direction : direction + 1, :], residue)
        residue = jnp.where(counted_ref[...] > slot, residue, 0.0)
        for earlier in found:
            residue = residue - earlier * jnp.sum(earlier * residue, axis=-1, keepdims=True)
        found.append(residue / jnp.sqrt(jnp.sum(residue * residue, axis=-1, keepdims=True) + EPSILON))
    for slot, vector in enumerate(found):
        for channel in range(chosen_ref.shape[0]):
            basis_ref[channel, slot : slot + 1, :] = vector[channel : channel + 1, :]

    own.wait()
    others = pl.ds(0, total - 1)
    pltpu.make_async_copy(pieces.at[others], pieces.at[others], send_sem).wait()
    pltpu.make_async_copy(dst_ref.at[others], dst_ref.at[others], recv_sem).wait()


def spectra(now, taps, steering, chosen, counted):
    extents = (16, 4, 4, 2)
    near = [8]
    for d in range(1, 8):
        near += [d, 16 - d]
    near.append(0)

    def kernel(*refs):
        spectra_kernel(extents, near, *refs)

    frames, rows, _ = now.shape
    tap_count = taps.shape[0]
    w1 = np.stack(first_stage_matrix())
    w2 = second_stage_matrix()
    table = twiddles()
    vmem = pl.BlockSpec(memory_space=pltpu.VMEM)
    anywhere = pl.BlockSpec(memory_space=pl.ANY)
    dma = pltpu.SemaphoreType.DMA
    return pl.pallas_call(
        kernel,
        out_shape=(
            jax.ShapeDtypeStruct((512, 8, FAST), BF16),
            jax.ShapeDtypeStruct((chosen.shape[0], chosen.shape[1], FAST), F32),
        ),
        in_specs=[anywhere, vmem, anywhere, anywhere, anywhere, vmem, vmem, vmem],
        out_specs=(vmem, vmem),
        scratch_shapes=[
            pltpu.VMEM((frames + tap_count - 1, rows, FAST), BF16),
            pltpu.VMEM((frames + tap_count - 1, rows, FAST), F32),
            pltpu.VMEM((tap_count, rows, FAST), F32),
            pltpu.VMEM((8, rows, FAST), F32),
            pltpu.VMEM((SLOW + 2, 2 * frames, FAST), F32),
            pltpu.VMEM((512, FAST), F32),
            pltpu.VMEM((512, 8, FAST), BF16),
            pltpu.VMEM(w1.shape, BF16),
            pltpu.VMEM(w2.shape, BF16),
            pltpu.VMEM(table.shape, F32),
            dma((frames // 16,)),
            dma((3,)),
            dma,
            dma,
            dma,
            dma,
            dma,
            pltpu.SemaphoreType.REGULAR,
            pltpu.SemaphoreType.REGULAR,
        ],
        compiler_params=pltpu.CompilerParams(collective_id=0, has_side_effects=True, vmem_limit_bytes=40 << 20),
        cost_estimate=pl.CostEstimate(flops=10**9, bytes_accessed=4 << 20, transcendentals=0),
    )(now, taps, jnp.asarray(w1), jnp.asarray(w2), jnp.asarray(table), steering, chosen, counted)


def covariance_kernel(frame_total, received_ref, basis_ref, out_ref, wide, rows):
    lane = lax.broadcasted_iota(jnp.int32, (64, FAST), 1)
    lower = lane < 64
    identity = (
        lax.broadcasted_iota(jnp.int32, (128, 128), 0) == lax.broadcasted_iota(jnp.int32, (128, 128), 1)
    ).astype(F32)
    shards = received_ref.shape[0] // 64
    for t in range(shards):
        wide[pl.ds(t * 512, 512), :] = received_ref[pl.ds(t * 64, 64)].astype(F32).reshape(512, FAST)
    for channel in range(4):
        for part in range(2):
            for t in range(0, shards, 2):
                a = wide[pl.ds(t * 512 + part * 4 + channel, 64, stride=8), :]
                b = wide[pl.ds((t + 1) * 512 + part * 4 + channel, 64, stride=8), :]
                first = jnp.where(lower, a, pltpu.roll(b, 64, 1))
                second = jnp.where(lower, pltpu.roll(a, 64, 1), b)
                rows[t // 2, pl.ds(part * 128, 64, stride=2), :] = first
                rows[t // 2, pl.ds(part * 128 + 1, 64, stride=2), :] = second
        x = jnp.concatenate([rows[i].astype(BF16) for i in range(shards // 2)], axis=1)
        outer = dot_t(x, x)
        gram_real = outer[:128, :128] + outer[128:, 128:]
        gram_imag = outer[128:, :128] - outer[:128, 128:]
        basis = basis_ref[channel]
        keep = identity - lax.dot_general(
            basis, basis, (((0,), (0,)), ((), ())), precision=HIGHEST, preferred_element_type=F32
        )
        left = jnp.dot(jnp.concatenate([gram_real, gram_imag], axis=0), keep, precision=HIGHEST, preferred_element_type=F32)
        both = jnp.concatenate([left[:128], left[128:]], axis=1)
        done = jnp.dot(keep, both, precision=HIGHEST, preferred_element_type=F32) * (1.0 / frame_total)
        out_ref[channel, 0] = done[:, :128]
        out_ref[channel, 1] = done[:, 128:]


def covariance(received, basis, frame_total):
    def kernel(*refs):
        covariance_kernel(frame_total, *refs)

    vmem = pl.BlockSpec(memory_space=pltpu.VMEM)
    return pl.pallas_call(
        kernel,
        out_shape=jax.ShapeDtypeStruct((4, 2, 128, 128), F32),
        in_specs=[vmem] * 2,
        out_specs=vmem,
        scratch_shapes=[pltpu.VMEM((4096, FAST), F32), pltpu.VMEM((4, 256, FAST), F32)],
        compiler_params=pltpu.CompilerParams(vmem_limit_bytes=24 << 20),
        cost_estimate=pl.CostEstimate(flops=10**9, bytes_accessed=2 << 20, transcendentals=0),
    )(received, basis)


def per_device(samples, taps, steering, interferer_ids, ranks):
    antennas, width = samples.shape
    tap_count, length = taps.shape
    frames = width // length
    peers = lax.axis_size("tm")
    blocks = samples.reshape(antennas, frames * SLOW, FAST).transpose(1, 0, 2).reshape(frames, SLOW * antennas, FAST)
    received, basis = spectra(
        blocks, taps.reshape(tap_count, SLOW, FAST), steering, interferer_ids, ranks.reshape(-1, 1)
    )
    return covariance(received, basis, frames * peers)


def solution(mesh):
    in_specs = (P("chan", "tm"), P(), P(), P(("chan", "tm"), None), P(("chan", "tm")))
    out_specs = P(("chan", "tm"), None, None, None)
    return jax.shard_map(per_device, mesh=mesh, in_specs=in_specs, out_specs=out_specs, check_vma=False)
```

```python
import jax
import jax.numpy as jnp
import numpy as np
from jax import lax
from jax.experimental import pallas as pl
from jax.experimental.pallas import tpu as pltpu
from jax.sharding import PartitionSpec as P

SLOW = 32
FAST = 128
EPSILON = 1e-06
F32 = jnp.float32
BF16 = jnp.bfloat16
HIGHEST = lax.Precision.HIGHEST


def split_constant(values):
    high = values.astype(np.float32).astype(jnp.bfloat16)
    low = (values - high.astype(np.float64)).astype(np.float32).astype(jnp.bfloat16)
    return high, low


def first_stage_matrix():
    p = np.arange(SLOW)
    rows = []
    for k1 in range(SLOW // 2 + 1):
        angle = 2.0 * np.pi * (k1 * p % SLOW) / SLOW
        rows.append(np.cos(angle))
        rows.append(-np.sin(angle) if k1 % (SLOW // 2) else np.zeros(SLOW))
    coefficients = np.stack(rows)
    full = np.einsum("kp,fg->kfgp", coefficients, np.eye(8)).reshape(len(rows) * 8, 8 * SLOW)
    return split_constant(full)


def second_stage_matrix():
    turns = np.outer(np.arange(64), np.arange(FAST)) % FAST
    angle = 2.0 * np.pi * turns / FAST
    real_rows = np.concatenate([np.cos(angle), np.sin(angle)], axis=1)
    imag_rows = np.concatenate([-np.sin(angle), np.cos(angle)], axis=1)
    high, low = split_constant(np.concatenate([real_rows, imag_rows], axis=0))
    return np.concatenate([high, low], axis=0)


def twiddles():
    angle = 2.0 * np.pi * np.outer(np.arange(SLOW), np.arange(FAST)) / (SLOW * FAST)
    sign = np.where(np.arange(SLOW) > SLOW // 2, -1.0, 1.0)[:, None]
    return np.stack([np.cos(angle), np.sin(angle), sign * np.cos(angle), sign * np.sin(angle)]).astype(np.float32)


def split(values):
    high = values.astype(BF16)
    return high, (values - high.astype(F32)).astype(BF16)


def dot(a, b):
    return lax.dot_general(a, b, (((1,), (0,)), ((), ())), preferred_element_type=F32)


def dot_t(a, b):
    return lax.dot_general(a, b, (((1,), (1,)), ((), ())), preferred_element_type=F32)


def covariance_kernel(extents, near, now_ref, taps_ref, w1_ref, w2_ref, table_ref, steering_ref, chosen_ref, counted_ref,
                      out_ref, arrived, window, taps, weights, filtered, y, spectrum, pieces, landed, wide, sides,
                      gram_ref, keep_ref, done, w1, w2, table, in_sem, const_sem, halo_send, halo_recv, send_sem, recv_sem,
                      line_sem, whole_sem, out_sem):
    nz, nx, ny, nc = extents
    nt = ny * nc
    groups = nz * nx
    tap_count = taps_ref.shape[0]
    halo = tap_count - 1
    frames, rows, _ = now_ref.shape
    channels, slots = chosen_ref.shape
    group = lax.axis_index("chan")
    shard = lax.axis_index("tm")
    z, x = group // nx, lax.rem(group, nx)

    def along_z(d):
        return {"chan": lax.rem(z + d, nz) * nx + x}

    def along_x(d):
        return {"chan": z * nx + lax.rem(x + d, nx)}

    def along_t(d):
        return {"tm": lax.rem(shard + d, nt)}

    constants = [
        pltpu.make_async_copy(source, target, const_sem.at[i])
        for i, (source, target) in enumerate(((taps_ref, taps), (w1_ref, w1), (w2_ref, w2), (table_ref, table)))
    ]
    inputs = [
        pltpu.make_async_copy(now_ref.at[pl.ds(i * 16, 16)], arrived.at[pl.ds(halo + i * 16, 16)], in_sem.at[i])
        for i in range(frames // 16)
    ]
    for copy in constants[:1] + inputs + constants[1:]:
        copy.start()

    barrier = pltpu.get_barrier_semaphore()
    for count, line in ((nz, along_z), (nt, along_t), (nx, along_x)):
        for d in range(1, count):
            pl.semaphore_signal(barrier, inc=1, device_id=line(d))

    @pl.when(shard == 0)
    def _():
        arrived[0:halo] = jnp.zeros((halo, rows, FAST), BF16)

    constants[0].wait()
    for p in range(SLOW):
        for t in range(0, tap_count, 8):
            tile = taps[t : t + 8, p * FAST : (p + 1) * FAST]
            for a in range(2):
                weights[pl.ds(t * rows + 2 * p + a, 8, stride=rows), :] = tile

    def widen(i):
        inputs[i].wait()

        def convert(g, carry):
            at = halo + i * 16 + g * 8
            window[pl.ds(at, 8)] = arrived[pl.ds(at, 8)].astype(F32)
            return carry

        lax.fori_loop(0, 2, convert, 0)

    def filter_group(g):
        for r in range(0, rows, 8):
            tap = [weights[t * rows + r : t * rows + r + 8, :] for t in range(tap_count)]
            seen = [window[g * 8 + i, r : r + 8, :] for i in range(8 + halo)]
            for f in range(8):
                result = tap[0] * seen[f]
                for t in range(1, tap_count):
                    result = result + tap[t] * seen[f + t]
                filtered[g % 2, f, r : r + 8, :] = result

    def turn_group(g):
        columns_h, columns_l = [], []
        for a in range(2):
            parts = [split(filtered[g % 2, f, pl.ds(a, SLOW, stride=2), :]) for f in range(8)]
            columns_h.append(jnp.concatenate([h for h, _ in parts], axis=0))
            columns_l.append(jnp.concatenate([l for _, l in parts], axis=0))
        xh = jnp.concatenate(columns_h, axis=1)
        xl = jnp.concatenate(columns_l, axis=1)
        size = (SLOW + 2) * 8
        both = dot(w1[...], xh)
        turned = both[:size] + both[size:] + dot(w1[:size], xl)
        for a in range(2):
            piece = turned[:, a * FAST : (a + 1) * FAST].reshape(SLOW + 2, 8, FAST)
            y[:, a * frames + g * 8 : a * frames + g * 8 + 8, :] = piece

    widen(0)
    widen(1)
    filter_group(2)
    constants[1].wait()
    widen(2)
    filter_group(3)
    turn_group(2)
    widen(3)

    pl.semaphore_wait(barrier, nz + nx + nt - 3)
    carried = pltpu.make_async_remote_copy(
        src_ref=now_ref.at[pl.ds(frames - halo, halo)],
        dst_ref=arrived.at[pl.ds(0, halo)],
        send_sem=halo_send,
        recv_sem=halo_recv,
        device_id=along_t(1),
    )

    @pl.when(shard < nt - 1)
    def _():
        carried.start()

    for d in range(1, nt):
        pl.semaphore_signal(line_sem, inc=1, device_id=along_t(d))

    filter_group(4)
    turn_group(3)
    filter_group(5)
    turn_group(4)
    pl.semaphore_wait(line_sem, nt - 1)
    for d in range(1, nx):
        pl.semaphore_signal(whole_sem, inc=1, device_id=along_x(d))
    filter_group(6)
    turn_group(5)
    filter_group(7)
    turn_group(6)

    @pl.when(shard > 0)
    def _():
        carried.wait_recv()

    @pl.when(shard < nt - 1)
    def _():
        carried.wait_send()

    window[0:halo] = arrived[0:halo].astype(F32)
    filter_group(0)
    turn_group(7)
    filter_group(1)
    turn_group(0)
    turn_group(1)
    pl.semaphore_wait(whole_sem, nx - 1)
    constants[2].wait()
    constants[3].wait()
    own = pltpu.make_async_copy(pieces.at[group], landed.at[group], recv_sem.at[0])

    def finish(i, carry):
        to_shard = lax.rem(shard + i, nt)
        for sub in range(4):
            k1 = to_shard * 4 + sub
            j = jnp.minimum(k1, SLOW - k1)
            real, imag = y[2 * j], y[2 * j + 1]
            cos, sin, signed_cos, signed_sin = (table[n, pl.ds(k1, 1), :] for n in range(4))
            zr = real * cos + imag * signed_sin
            zi = imag * signed_cos - real * sin
            zh, zl = split(jnp.concatenate([zr, zi], axis=1))
            both = dot_t(w2[...], zh)
            result = both[:FAST] + both[FAST:] + dot_t(w2[:FAST], zl)
            for part in range(2):
                spectrum[pl.ds(part * 4 + sub, 64, stride=8), :] = result[part * 64 : (part + 1) * 64]
        base = pl.multiple_of(i * groups, groups)
        pieces[pl.ds(base, groups)] = spectrum[...].reshape(groups, 8, FAST).astype(BF16)

        def send(dz, dx):
            to_group = lax.rem(z + dz, nz) * nx + lax.rem(x + dx, nx)
            pltpu.make_async_remote_copy(
                src_ref=pieces.at[base + to_group],
                dst_ref=landed.at[base + group],
                send_sem=send_sem,
                recv_sem=recv_sem.at[i],
                device_id={"chan": to_group, "tm": to_shard},
            ).start()

        def column(dx, inner):
            for dz in near:
                if dz:
                    send(dz, dx)
                else:

                    @pl.when(i + dx > 0)
                    def _():
                        send(0, dx)

                    @pl.when(i + dx == 0)
                    def _():
                        own.start()

            return inner

        lax.fori_loop(0, nx, column, 0)
        return carry

    lax.fori_loop(0, nt, finish, 0)

    row = lax.broadcasted_iota(jnp.int32, (channels, FAST), 0)
    counted = jnp.zeros((channels, FAST), jnp.int32)
    for channel in range(channels):
        counted = jnp.where(row == channel, counted_ref[channel], counted)
    found = []
    for slot in range(slots):
        wanted = chosen_ref[:, slot : slot + 1]
        residue = jnp.zeros((channels, FAST), F32)
        for direction in range(steering_ref.shape[0]):
            residue = jnp.where(wanted == direction, steering_ref[direction : direction + 1, :], residue)
        residue = jnp.where(counted > slot, residue, 0.0)
        for earlier in found:
            residue = residue - earlier * jnp.sum(earlier * residue, axis=-1, keepdims=True)
        found.append(residue / jnp.sqrt(jnp.sum(residue * residue, axis=-1, keepdims=True) + EPSILON))
    identity = (
        lax.broadcasted_iota(jnp.int32, (FAST, FAST), 0) == lax.broadcasted_iota(jnp.int32, (FAST, FAST), 1)
    ).astype(F32)
    for channel in range(channels):
        basis = jnp.concatenate([vector[channel : channel + 1, :] for vector in found], axis=0)
        keep_ref[channel] = identity - lax.dot_general(
            basis, basis, (((0,), (0,)), ((), ())), precision=HIGHEST, preferred_element_type=F32
        )

    gram_ref[...] = jnp.zeros(gram_ref.shape, F32)
    lower = lax.broadcasted_iota(jnp.int32, (groups, FAST), 1) < frames

    def gather(pair):
        for which in range(2):
            part = landed.at[pl.ds((2 * pair + which) * groups, groups)]
            pltpu.make_async_copy(part, part, recv_sem.at[2 * pair + which]).wait()
            wide[which * 8 * groups : (which + 1) * 8 * groups, :] = part[...].astype(F32).reshape(8 * groups, FAST)
        for channel in range(channels):
            for half in range(2):
                first = wide[pl.ds(half * 4 + channel, groups, stride=8), :]
                second = wide[pl.ds(8 * groups + half * 4 + channel, groups, stride=8), :]
                sides[channel, pl.ds(half * FAST, groups, stride=2), :] = jnp.where(
                    lower, first, pltpu.roll(second, frames, 1)
                )
                sides[channel, pl.ds(half * FAST + 1, groups, stride=2), :] = jnp.where(
                    lower, pltpu.roll(first, frames, 1), second
                )
            side = sides[channel].astype(BF16)
            outer = dot_t(side, side)
            gram_ref[channel, :FAST] += outer[:FAST, :FAST] + outer[FAST:, FAST:]
            gram_ref[channel, FAST:] += outer[FAST:, :FAST] - outer[:FAST, FAST:]

    def early(pair, carry):
        gather(pair)
        return carry

    lax.fori_loop(0, nt // 2 - 1, early, 0)
    others = pl.ds(0, nt * groups - 1)
    pltpu.make_async_copy(pieces.at[others], pieces.at[others], send_sem).wait()
    gather(nt // 2 - 1)
    copies = []
    for channel in range(channels):
        keep = keep_ref[channel]
        left = jnp.dot(gram_ref[channel], keep, precision=HIGHEST, preferred_element_type=F32)
        both = jnp.concatenate([left[:FAST], left[FAST:]], axis=1)
        result = jnp.dot(keep, both, precision=HIGHEST, preferred_element_type=F32) * (1.0 / (frames * nt))
        done[channel, 0] = result[:, :FAST]
        done[channel, 1] = result[:, FAST:]
        copies.append(pltpu.make_async_copy(done.at[channel], out_ref.at[channel], out_sem.at[channel]))
        copies[-1].start()
    for copy in copies:
        copy.wait()


def covariance(now, taps, steering, chosen, counted):
    extents = (16, 4, 4, 2)
    near = [8]
    for d in range(1, 8):
        near += [d, 16 - d]
    near.append(0)

    def kernel(*refs):
        covariance_kernel(extents, near, *refs)

    frames, rows, _ = now.shape
    tap_count, length = taps.shape
    channels = chosen.shape[0]
    w1 = np.concatenate(first_stage_matrix(), axis=0)
    w2 = second_stage_matrix()
    table = twiddles()
    vmem = pl.BlockSpec(memory_space=pltpu.VMEM)
    hbm = pl.BlockSpec(memory_space=pltpu.HBM)
    smem = pl.BlockSpec(memory_space=pltpu.SMEM)
    dma = pltpu.SemaphoreType.DMA
    return pl.pallas_call(
        kernel,
        out_shape=jax.ShapeDtypeStruct((channels, 2, FAST, FAST), F32),
        in_specs=[hbm, hbm, hbm, hbm, hbm, vmem, vmem, smem],
        out_specs=hbm,
        scratch_shapes=[
            pltpu.VMEM((frames + tap_count - 1, rows, FAST), BF16),
            pltpu.VMEM((frames + tap_count - 1, rows, FAST), F32),
            pltpu.VMEM((tap_count, length), F32),
            pltpu.VMEM((tap_count * rows, FAST), F32),
            pltpu.VMEM((2, 8, rows, FAST), F32),
            pltpu.VMEM((SLOW + 2, 2 * frames, FAST), F32),
            pltpu.VMEM((512, FAST), F32),
            pltpu.VMEM((512, 8, FAST), BF16),
            pltpu.VMEM((512, 8, FAST), BF16),
            pltpu.VMEM((1024, FAST), F32),
            pltpu.VMEM((channels, 2 * FAST, FAST), F32),
            pltpu.VMEM((channels, 2 * FAST, FAST), F32),
            pltpu.VMEM((channels, FAST, FAST), F32),
            pltpu.VMEM((channels, 2, FAST, FAST), F32),
            pltpu.VMEM(w1.shape, BF16),
            pltpu.VMEM(w2.shape, BF16),
            pltpu.VMEM(table.shape, F32),
            dma((frames // 16,)),
            dma((4,)),
            dma,
            dma,
            dma,
            dma((8,)),
            pltpu.SemaphoreType.REGULAR,
            pltpu.SemaphoreType.REGULAR,
            dma((channels,)),
        ],
        compiler_params=pltpu.CompilerParams(collective_id=0, has_side_effects=True, vmem_limit_bytes=60 << 20),
        cost_estimate=pl.CostEstimate(flops=10**9, bytes_accessed=4 << 20, transcendentals=0),
    )(now, taps, jnp.asarray(w1), jnp.asarray(w2), jnp.asarray(table), steering, chosen, counted)


def per_device(samples, taps, steering, interferer_ids, ranks):
    antennas, width = samples.shape
    length = taps.shape[1]
    frames = width // length
    blocks = samples.reshape(antennas, frames * SLOW, FAST).transpose(1, 0, 2).reshape(frames, SLOW * antennas, FAST)
    return covariance(blocks, taps, steering, interferer_ids, ranks)


def solution(mesh):
    in_specs = (P("chan", "tm"), P(), P(), P(("chan", "tm"), None), P(("chan", "tm")))
    out_specs = P(("chan", "tm"), None, None, None)
    return jax.shard_map(per_device, mesh=mesh, in_specs=in_specs, out_specs=out_specs, check_vma=False)
```

```python
import jax
import jax.numpy as jnp
import numpy as np
from jax import lax
from jax.experimental import pallas as pl
from jax.experimental.pallas import tpu as pltpu
from jax.sharding import PartitionSpec as P

SLOW = 32
FAST = 128
EPSILON = 1e-06
F32 = jnp.float32
BF16 = jnp.bfloat16
HIGHEST = lax.Precision.HIGHEST


def split_constant(values):
    high = values.astype(np.float32).astype(jnp.bfloat16)
    low = (values - high.astype(np.float64)).astype(np.float32).astype(jnp.bfloat16)
    return high, low


def first_stage_matrix():
    p = np.arange(SLOW)
    rows = []
    for k1 in range(SLOW // 2 + 1):
        angle = 2.0 * np.pi * (k1 * p % SLOW) / SLOW
        rows.append(np.cos(angle))
        rows.append(-np.sin(angle) if k1 % (SLOW // 2) else np.zeros(SLOW))
    coefficients = np.stack(rows)
    full = np.einsum("kp,fg->kfgp", coefficients, np.eye(8)).reshape(len(rows) * 8, 8 * SLOW)
    return split_constant(full)


def second_stage_matrix():
    turns = np.outer(np.arange(64), np.arange(FAST)) % FAST
    angle = 2.0 * np.pi * turns / FAST
    real_rows = np.concatenate([np.cos(angle), np.sin(angle)], axis=1)
    imag_rows = np.concatenate([-np.sin(angle), np.cos(angle)], axis=1)
    high, low = split_constant(np.concatenate([real_rows, imag_rows], axis=0))
    return np.concatenate([high, low], axis=0)


def twiddles():
    angle = 2.0 * np.pi * np.outer(np.arange(SLOW), np.arange(FAST)) / (SLOW * FAST)
    sign = np.where(np.arange(SLOW) > SLOW // 2, -1.0, 1.0)[:, None]
    return np.stack([np.cos(angle), np.sin(angle), sign * np.cos(angle), sign * np.sin(angle)]).astype(np.float32)


def split(values):
    high = values.astype(BF16)
    return high, (values - high.astype(F32)).astype(BF16)


def dot(a, b):
    return lax.dot_general(a, b, (((1,), (0,)), ((), ())), preferred_element_type=F32)


def dot_t(a, b):
    return lax.dot_general(a, b, (((1,), (1,)), ((), ())), preferred_element_type=F32)


def covariance_kernel(extents, near, now_ref, taps_ref, w1_ref, w2_ref, table_ref, steering_ref, chosen_ref, counted_ref,
                      out_ref, arrived, window, taps, weights, even, odd, y, spectrum, pieces, landed, wide, sides,
                      gram_ref, keep_ref, done, w1, w2, table, in_sem, const_sem, halo_send, halo_recv, send_sem, recv_sem,
                      plane_sem, whole_sem, out_sem):
    nz, nx, ny, nc = extents
    nt = ny * nc
    groups = nz * nx
    tap_count = taps_ref.shape[0]
    halo = tap_count - 1
    frames, rows, _ = now_ref.shape
    channels, slots = chosen_ref.shape
    group = lax.axis_index("chan")
    shard = lax.axis_index("tm")
    z, x = group // nx, lax.rem(group, nx)

    def along_z(d):
        return {"chan": lax.rem(z + d, nz) * nx + x}

    def along_x(d):
        return {"chan": z * nx + lax.rem(x + d, nx)}

    def along_t(d):
        return {"tm": lax.rem(shard + d, nt)}

    constants = [
        pltpu.make_async_copy(source, target, const_sem.at[i])
        for i, (source, target) in enumerate(((taps_ref, taps), (w1_ref, w1), (w2_ref, w2), (table_ref, table)))
    ]
    inputs = [
        pltpu.make_async_copy(now_ref.at[pl.ds(i * 16, 16)], arrived.at[pl.ds(halo + i * 16, 16)], in_sem.at[i])
        for i in range(frames // 16)
    ]
    for copy in constants[:1] + inputs + constants[1:]:
        copy.start()

    barrier = pltpu.get_barrier_semaphore()
    for d in near[:-1]:
        pl.semaphore_signal(barrier, inc=1, device_id=along_z(d))
    for count, line in ((nt, along_t), (nx, along_x)):
        for d in range(1, count):
            pl.semaphore_signal(barrier, inc=1, device_id=line(d))

    @pl.when(shard == 0)
    def _():
        arrived[0:halo] = jnp.zeros((halo, rows, FAST), BF16)

    constants[0].wait()
    for p in range(SLOW):
        for t in range(0, tap_count, 8):
            tile = taps[t : t + 8, p * FAST : (p + 1) * FAST]
            for a in range(2):
                weights[pl.ds(t * rows + 2 * p + a, 8, stride=rows), :] = tile

    def widen(first, last):
        window[first:last] = arrived[first:last].astype(F32)

    def widen_group(g):
        if g % 2 == 0:
            inputs[g // 2].wait()
        widen(halo + g * 8, halo + g * 8 + 8)

    def filter_group(g, filtered):
        for r in range(0, rows, 8):
            tap = [weights[t * rows + r : t * rows + r + 8, :] for t in range(tap_count)]
            seen = [window[g * 8 + i, r : r + 8, :] for i in range(8 + halo)]
            for f in range(8):
                result = tap[0] * seen[f]
                for t in range(1, tap_count):
                    result = result + tap[t] * seen[f + t]
                filtered[f, r : r + 8, :] = result

    def turn_group(g, filtered):
        columns_h, columns_l = [], []
        for a in range(2):
            parts = [split(filtered[f, pl.ds(a, SLOW, stride=2), :]) for f in range(8)]
            columns_h.append(jnp.concatenate([h for h, _ in parts], axis=0))
            columns_l.append(jnp.concatenate([l for _, l in parts], axis=0))
        xh = jnp.concatenate(columns_h, axis=1)
        xl = jnp.concatenate(columns_l, axis=1)
        size = (SLOW + 2) * 8
        both = dot(w1[...], xh)
        turned = both[:size] + both[size:] + dot(w1[:size], xl)
        for a in range(2):
            piece = turned[:, a * FAST : (a + 1) * FAST].reshape(SLOW + 2, 8, FAST)
            y[:, a * frames + g * 8 : a * frames + g * 8 + 8, :] = piece

    for g in range(3):
        widen_group(g)
    filter_group(2, even)
    constants[1].wait()
    widen_group(3)
    filter_group(3, odd)
    turn_group(2, even)

    pl.semaphore_wait(barrier, nz + nx + nt - 3)
    near_halo = halo // 2
    carried = [
        pltpu.make_async_remote_copy(
            src_ref=now_ref.at[pl.ds(frames - halo + first, count)],
            dst_ref=arrived.at[pl.ds(first, count)],
            send_sem=halo_send.at[i],
            recv_sem=halo_recv.at[i],
            device_id=along_t(1),
        )
        for i, (first, count) in enumerate(((halo - near_halo, near_halo), (0, halo - near_halo)))
    ]

    @pl.when(shard < nt - 1)
    def _():
        for copy in carried:
            copy.start()

    for d in range(1, nx):
        pl.semaphore_signal(plane_sem, inc=1, device_id=along_x(d))

    for g in range(4, 8):
        widen_group(g)
        filter_group(g, odd if g % 2 else even)
        turn_group(g - 1, even if g % 2 else odd)

    @pl.when(shard > 0)
    def _():
        carried[0].wait_recv()

    widen(halo - near_halo, halo)
    filter_group(1, even)
    turn_group(7, odd)

    @pl.when(shard > 0)
    def _():
        carried[1].wait_recv()

    widen(0, halo - near_halo)
    filter_group(0, odd)
    turn_group(1, even)
    turn_group(0, odd)
    constants[2].wait()
    constants[3].wait()

    def finish(i):
        to_shard = lax.rem(shard + i, nt)
        for sub in range(4):
            k1 = to_shard * 4 + sub
            j = jnp.minimum(k1, SLOW - k1)
            real, imag = y[2 * j], y[2 * j + 1]
            cos, sin, signed_cos, signed_sin = (table[n, pl.ds(k1, 1), :] for n in range(4))
            zr = real * cos + imag * signed_sin
            zi = imag * signed_cos - real * sin
            zh, zl = split(jnp.concatenate([zr, zi], axis=1))
            both = dot_t(w2[...], zh)
            result = both[:FAST] + both[FAST:] + dot_t(w2[:FAST], zl)
            for part in range(2):
                spectrum[pl.ds(part * 4 + sub, 64, stride=8), :] = result[part * 64 : (part + 1) * 64]
        base = pl.multiple_of(i * groups, groups)
        pieces[pl.ds(base, groups)] = spectrum[...].reshape(groups, 8, FAST).astype(BF16)

    def send(i, dz, dx):
        to_shard = lax.rem(shard + i, nt)
        to_group = lax.rem(z + dz, nz) * nx + lax.rem(x + dx, nx)
        pltpu.make_async_remote_copy(
            src_ref=pieces.at[i * groups + to_group],
            dst_ref=landed.at[i * groups + group],
            send_sem=send_sem,
            recv_sem=recv_sem.at[i],
            device_id={"chan": to_group, "tm": to_shard},
        ).start()

    def columns(i, first):
        def column(dx, carry):
            for dz in near:
                send(i, dz, dx)
            return carry

        lax.fori_loop(first, nx, column, 0)

    zero = jnp.int32(0)
    finish(zero)
    for dz in near[:-1]:
        send(zero, dz, 0)
    pltpu.make_async_copy(pieces.at[group], landed.at[group], recv_sem.at[0]).start()
    pl.semaphore_wait(plane_sem, nx - 1)
    for d in range(1, nt):
        pl.semaphore_signal(whole_sem, inc=1, device_id=along_t(d))
    columns(zero, 1)
    pl.semaphore_wait(whole_sem, nt - 1)

    def onward(i, carry):
        finish(i)
        columns(i, 0)
        return carry

    lax.fori_loop(1, nt, onward, 0)

    row = lax.broadcasted_iota(jnp.int32, (channels, FAST), 0)
    counted = jnp.zeros((channels, FAST), jnp.int32)
    for channel in range(channels):
        counted = jnp.where(row == channel, counted_ref[channel], counted)
    found = []
    for slot in range(slots):
        wanted = chosen_ref[:, slot : slot + 1]
        residue = jnp.zeros((channels, FAST), F32)
        for direction in range(steering_ref.shape[0]):
            residue = jnp.where(wanted == direction, steering_ref[direction : direction + 1, :], residue)
        residue = jnp.where(counted > slot, residue, 0.0)
        for earlier in found:
            residue = residue - earlier * jnp.sum(earlier * residue, axis=-1, keepdims=True)
        found.append(residue / jnp.sqrt(jnp.sum(residue * residue, axis=-1, keepdims=True) + EPSILON))
    identity = (
        lax.broadcasted_iota(jnp.int32, (FAST, FAST), 0) == lax.broadcasted_iota(jnp.int32, (FAST, FAST), 1)
    ).astype(F32)
    for channel in range(channels):
        basis = jnp.concatenate([vector[channel : channel + 1, :] for vector in found], axis=0)
        keep = identity - lax.dot_general(
            basis, basis, (((0,), (0,)), ((), ())), precision=HIGHEST, preferred_element_type=F32
        )
        keep_ref[channel, :FAST], keep_ref[channel, FAST:] = split(keep)

    gram_ref[...] = jnp.zeros(gram_ref.shape, F32)
    lower = lax.broadcasted_iota(jnp.int32, (groups, FAST), 1) < frames

    def gather(pair):
        for which in range(2):
            part = landed.at[pl.ds((2 * pair + which) * groups, groups)]
            pltpu.make_async_copy(part, part, recv_sem.at[2 * pair + which]).wait()
            wide[which * 8 * groups : (which + 1) * 8 * groups, :] = part[...].astype(F32).reshape(8 * groups, FAST)
        for channel in range(channels):
            for half in range(2):
                first = wide[pl.ds(half * 4 + channel, groups, stride=8), :]
                second = wide[pl.ds(8 * groups + half * 4 + channel, groups, stride=8), :]
                sides[channel, pl.ds(half * FAST, groups, stride=2), :] = jnp.where(
                    lower, first, pltpu.roll(second, frames, 1)
                )
                sides[channel, pl.ds(half * FAST + 1, groups, stride=2), :] = jnp.where(
                    lower, pltpu.roll(first, frames, 1), second
                )
            side = sides[channel].astype(BF16)
            outer = dot_t(side, side)
            gram_ref[channel, :FAST] += outer[:FAST, :FAST] + outer[FAST:, FAST:]
            gram_ref[channel, FAST:] += outer[FAST:, :FAST] - outer[:FAST, FAST:]

    def early(pair, carry):
        gather(pair)
        return carry

    lax.fori_loop(0, nt // 2 - 1, early, 0)
    others = pl.ds(0, nt * groups - 1)
    pltpu.make_async_copy(pieces.at[others], pieces.at[others], send_sem).wait()

    @pl.when(shard < nt - 1)
    def _():
        for copy in carried:
            copy.wait_send()

    gather(nt // 2 - 1)
    copies = []
    for channel in range(channels):
        keep_h, keep_l = keep_ref[channel, :FAST], keep_ref[channel, FAST:]
        gram_h, gram_l = split(gram_ref[channel])
        left = dot(gram_h, keep_h) + dot(gram_l, keep_h) + dot(gram_h, keep_l)
        left_h, left_l = split(jnp.concatenate([left[:FAST], left[FAST:]], axis=1))
        result = (dot(keep_h, left_h) + dot(keep_h, left_l) + dot(keep_l, left_h)) * (1.0 / (frames * nt))
        done[channel, 0] = result[:, :FAST]
        done[channel, 1] = result[:, FAST:]
        copies.append(pltpu.make_async_copy(done.at[channel], out_ref.at[channel], out_sem.at[channel]))
        copies[-1].start()
    for copy in copies:
        copy.wait()


def covariance(now, taps, steering, chosen, counted):
    extents = (16, 4, 4, 2)
    near = [8]
    for d in range(7, 0, -1):
        near += [d, 16 - d]
    near.append(0)

    def kernel(*refs):
        covariance_kernel(extents, near, *refs)

    frames, rows, _ = now.shape
    tap_count, length = taps.shape
    channels = chosen.shape[0]
    w1 = np.concatenate(first_stage_matrix(), axis=0)
    w2 = second_stage_matrix()
    table = twiddles()
    vmem = pl.BlockSpec(memory_space=pltpu.VMEM)
    hbm = pl.BlockSpec(memory_space=pltpu.HBM)
    smem = pl.BlockSpec(memory_space=pltpu.SMEM)
    dma = pltpu.SemaphoreType.DMA
    return pl.pallas_call(
        kernel,
        out_shape=jax.ShapeDtypeStruct((channels, 2, FAST, FAST), F32),
        in_specs=[hbm, hbm, hbm, hbm, hbm, vmem, vmem, smem],
        out_specs=hbm,
        scratch_shapes=[
            pltpu.VMEM((frames + tap_count - 1, rows, FAST), BF16),
            pltpu.VMEM((frames + tap_count - 1, rows, FAST), F32),
            pltpu.VMEM((tap_count, length), F32),
            pltpu.VMEM((tap_count * rows, FAST), F32),
            pltpu.VMEM((8, rows, FAST), F32),
            pltpu.VMEM((8, rows, FAST), F32),
            pltpu.VMEM((SLOW + 2, 2 * frames, FAST), F32),
            pltpu.VMEM((512, FAST), F32),
            pltpu.VMEM((512, 8, FAST), BF16),
            pltpu.VMEM((512, 8, FAST), BF16),
            pltpu.VMEM((1024, FAST), F32),
            pltpu.VMEM((channels, 2 * FAST, FAST), F32),
            pltpu.VMEM((channels, 2 * FAST, FAST), F32),
            pltpu.VMEM((channels, 2 * FAST, FAST), BF16),
            pltpu.VMEM((channels, 2, FAST, FAST), F32),
            pltpu.VMEM(w1.shape, BF16),
            pltpu.VMEM(w2.shape, BF16),
            pltpu.VMEM(table.shape, F32),
            dma((frames // 16,)),
            dma((4,)),
            dma((2,)),
            dma((2,)),
            dma,
            dma((8,)),
            pltpu.SemaphoreType.REGULAR,
            pltpu.SemaphoreType.REGULAR,
            dma((channels,)),
        ],
        compiler_params=pltpu.CompilerParams(collective_id=0, has_side_effects=True, vmem_limit_bytes=60 << 20),
        cost_estimate=pl.CostEstimate(flops=10**9, bytes_accessed=4 << 20, transcendentals=0),
    )(now, taps, jnp.asarray(w1), jnp.asarray(w2), jnp.asarray(table), steering, chosen, counted)


def per_device(samples, taps, steering, interferer_ids, ranks):
    antennas, width = samples.shape
    length = taps.shape[1]
    frames = width // length
    blocks = samples.reshape(antennas, frames * SLOW, FAST).transpose(1, 0, 2).reshape(frames, SLOW * antennas, FAST)
    return covariance(blocks, taps, steering, interferer_ids, ranks)


def solution(mesh):
    in_specs = (P("chan", "tm"), P(), P(), P(("chan", "tm"), None), P(("chan", "tm")))
    out_specs = P(("chan", "tm"), None, None, None)
    return jax.shard_map(per_device, mesh=mesh, in_specs=in_specs, out_specs=out_specs, check_vma=False)
```

```python
import jax
import jax.numpy as jnp
import numpy as np
from jax import lax
from jax.experimental import pallas as pl
from jax.experimental.pallas import tpu as pltpu
from jax.sharding import PartitionSpec as P

SLOW = 32
FAST = 128
EPSILON = 1e-06
F32 = jnp.float32
BF16 = jnp.bfloat16
HIGHEST = lax.Precision.HIGHEST


def split_constant(values):
    high = values.astype(np.float32).astype(jnp.bfloat16)
    low = (values - high.astype(np.float64)).astype(np.float32).astype(jnp.bfloat16)
    return high, low


def first_stage_matrix():
    p = np.arange(SLOW)
    rows = []
    for k1 in range(SLOW // 2 + 1):
        angle = 2.0 * np.pi * (k1 * p % SLOW) / SLOW
        rows.append(np.cos(angle))
        rows.append(-np.sin(angle) if k1 % (SLOW // 2) else np.zeros(SLOW))
    coefficients = np.stack(rows)
    full = np.einsum("kp,fg->kfgp", coefficients, np.eye(8)).reshape(len(rows) * 8, 8 * SLOW)
    return split_constant(full)


def second_stage_matrix():
    turns = np.outer(np.arange(64), np.arange(FAST)) % FAST
    angle = 2.0 * np.pi * turns / FAST
    real_rows = np.concatenate([np.cos(angle), np.sin(angle)], axis=1)
    imag_rows = np.concatenate([-np.sin(angle), np.cos(angle)], axis=1)
    return split_constant(np.concatenate([real_rows, imag_rows], axis=0))


def twiddles():
    angle = 2.0 * np.pi * np.outer(np.arange(SLOW), np.arange(FAST)) / (SLOW * FAST)
    sign = np.where(np.arange(SLOW) > SLOW // 2, -1.0, 1.0)[:, None]
    return np.stack([np.cos(angle), np.sin(angle), sign * np.cos(angle), sign * np.sin(angle)]).astype(np.float32)


def split(values):
    high = values.astype(BF16)
    return high, (values - high.astype(F32)).astype(BF16)


def beside(high, low, axis):
    return jnp.concatenate([high, low, high], axis=axis)


def dot(a, b):
    return lax.dot_general(a, b, (((1,), (0,)), ((), ())), preferred_element_type=F32)


def dot_t(a, b):
    return lax.dot_general(a, b, (((1,), (1,)), ((), ())), preferred_element_type=F32)


def covariance_kernel(extents, near, now_ref, taps_ref, w1_ref, w2_ref, table_ref, steering_ref, chosen_ref, counted_ref,
                      out_ref, arrived, window, taps, weights, even, odd, y, spectrum, pieces, landed, wide, sides,
                      gram_ref, below, aside, steering, chosen, counted_scalar, w1, w2, table, in_sem, const_sem, halo_send, halo_recv, send_sem, recv_sem,
                      plane_sem, whole_sem):
    nz, nx, ny, nc = extents
    nt = ny * nc
    groups = nz * nx
    tap_count = taps_ref.shape[0]
    halo = tap_count - 1
    frames, rows, _ = now_ref.shape
    channels, slots = chosen_ref.shape
    group = lax.axis_index("chan")
    shard = lax.axis_index("tm")
    z, x = group // nx, lax.rem(group, nx)

    def along_z(d):
        return {"chan": lax.rem(z + d, nz) * nx + x}

    def along_x(d):
        return {"chan": z * nx + lax.rem(x + d, nx)}

    def along_t(d):
        return {"tm": lax.rem(shard + d, nt)}

    pairs = (
        (taps_ref, taps),
        (w1_ref, w1),
        (w2_ref, w2),
        (table_ref, table),
        (steering_ref, steering),
        (chosen_ref, chosen),
        (counted_ref, counted_scalar),
    )
    constants = [
        pltpu.make_async_copy(source, target, const_sem.at[i])
        for i, (source, target) in enumerate(pairs)
    ]
    inputs = [
        pltpu.make_async_copy(now_ref.at[pl.ds(i * 16, 16)], arrived.at[pl.ds(halo + i * 16, 16)], in_sem.at[i])
        for i in range(frames // 16)
    ]
    for copy in constants[:1] + inputs + constants[1:]:
        copy.start()

    barrier = pltpu.get_barrier_semaphore()
    for d in near[:-1]:
        pl.semaphore_signal(barrier, inc=1, device_id=along_z(d))
    for count, line in ((nt, along_t), (nx, along_x)):
        for d in range(1, count):
            pl.semaphore_signal(barrier, inc=1, device_id=line(d))

    @pl.when(shard == 0)
    def _():
        arrived[0:halo] = jnp.zeros((halo, rows, FAST), BF16)

    constants[0].wait()
    for p in range(SLOW):
        for t in range(0, tap_count, 8):
            tile = taps[t : t + 8, p * FAST : (p + 1) * FAST]
            for a in range(2):
                weights[pl.ds(t * rows + 2 * p + a, 8, stride=rows), :] = tile

    def widen(first, last):
        window[first:last] = arrived[first:last].astype(F32)

    def widen_group(g):
        if g % 2 == 0:
            inputs[g // 2].wait()
        widen(halo + g * 8, halo + g * 8 + 8)

    def filter_group(g, filtered):
        for r in range(0, rows, 8):
            tap = [weights[t * rows + r : t * rows + r + 8, :] for t in range(tap_count)]
            seen = [window[g * 8 + i, r : r + 8, :] for i in range(8 + halo)]
            for f in range(8):
                result = tap[0] * seen[f]
                for t in range(1, tap_count):
                    result = result + tap[t] * seen[f + t]
                filtered[f, r : r + 8, :] = result

    def turn_group(g, filtered):
        columns_h, columns_l = [], []
        for a in range(2):
            parts = [split(filtered[f, pl.ds(a, SLOW, stride=2), :]) for f in range(8)]
            columns_h.append(jnp.concatenate([h for h, _ in parts], axis=0))
            columns_l.append(jnp.concatenate([l for _, l in parts], axis=0))
        xh = jnp.concatenate(columns_h, axis=1)
        xl = jnp.concatenate(columns_l, axis=1)
        turned = dot(w1[...], jnp.concatenate([xh, xh, xl], axis=0))
        for a in range(2):
            piece = turned[:, a * FAST : (a + 1) * FAST].reshape(SLOW + 2, 8, FAST)
            y[:, a * frames + g * 8 : a * frames + g * 8 + 8, :] = piece

    for g in range(3):
        widen_group(g)
    filter_group(2, even)
    constants[1].wait()
    widen_group(3)
    filter_group(3, odd)
    turn_group(2, even)

    pl.semaphore_wait(barrier, nz + nx + nt - 3)
    near_halo = halo // 2
    carried = [
        pltpu.make_async_remote_copy(
            src_ref=now_ref.at[pl.ds(frames - halo + first, count)],
            dst_ref=arrived.at[pl.ds(first, count)],
            send_sem=halo_send.at[i],
            recv_sem=halo_recv.at[i],
            device_id=along_t(1),
        )
        for i, (first, count) in enumerate(((halo - near_halo, near_halo), (0, halo - near_halo)))
    ]

    @pl.when(shard < nt - 1)
    def _():
        for copy in carried:
            copy.start()

    for d in range(1, nx):
        pl.semaphore_signal(plane_sem, inc=1, device_id=along_x(d))

    for g in range(4, 8):
        widen_group(g)
        filter_group(g, odd if g % 2 else even)
        turn_group(g - 1, even if g % 2 else odd)

    @pl.when(shard > 0)
    def _():
        carried[0].wait_recv()

    widen(halo - near_halo, halo)
    filter_group(1, even)
    turn_group(7, odd)

    @pl.when(shard > 0)
    def _():
        carried[1].wait_recv()

    widen(0, halo - near_halo)
    filter_group(0, odd)
    turn_group(1, even)
    turn_group(0, odd)
    for copy in constants[2:]:
        copy.wait()

    def finish(i):
        to_shard = lax.rem(shard + i, nt)
        for sub in range(4):
            k1 = to_shard * 4 + sub
            j = jnp.minimum(k1, SLOW - k1)
            real, imag = y[2 * j], y[2 * j + 1]
            cos, sin, signed_cos, signed_sin = (table[n, pl.ds(k1, 1), :] for n in range(4))
            zr = real * cos + imag * signed_sin
            zi = imag * signed_cos - real * sin
            zh, zl = split(jnp.concatenate([zr, zi], axis=1))
            result = dot_t(w2[...], jnp.concatenate([zh, zh, zl], axis=1))
            for part in range(2):
                spectrum[pl.ds(part * 4 + sub, 64, stride=8), :] = result[part * 64 : (part + 1) * 64]
        base = pl.multiple_of(i * groups, groups)
        pieces[pl.ds(base, groups)] = spectrum[...].reshape(groups, 8, FAST).astype(BF16)

    def send(i, dz, dx):
        to_shard = lax.rem(shard + i, nt)
        to_group = lax.rem(z + dz, nz) * nx + lax.rem(x + dx, nx)
        pltpu.make_async_remote_copy(
            src_ref=pieces.at[i * groups + to_group],
            dst_ref=landed.at[i * groups + group],
            send_sem=send_sem,
            recv_sem=recv_sem.at[i],
            device_id={"chan": to_group, "tm": to_shard},
        ).start()

    def columns(i, first):
        def column(dx, carry):
            for dz in near:
                send(i, dz, dx)
            return carry

        lax.fori_loop(first, nx, column, 0)

    zero = jnp.int32(0)
    finish(zero)
    for dz in near[:-1]:
        send(zero, dz, 0)
    pltpu.make_async_copy(pieces.at[group], landed.at[group], recv_sem.at[0]).start()
    pl.semaphore_wait(plane_sem, nx - 1)
    for d in range(1, nt):
        pl.semaphore_signal(whole_sem.at[nt - d], inc=1, device_id=along_t(d))
    columns(zero, 1)

    def onward(i, carry):
        finish(i)
        pl.semaphore_wait(whole_sem.at[i], 1)
        columns(i, 0)
        return carry

    lax.fori_loop(1, nt, onward, 0)

    row = lax.broadcasted_iota(jnp.int32, (channels, FAST), 0)
    counted = jnp.zeros((channels, FAST), jnp.int32)
    for channel in range(channels):
        counted = jnp.where(row == channel, counted_scalar[channel], counted)
    found = []
    for slot in range(slots):
        wanted = chosen[:, slot : slot + 1]
        residue = jnp.zeros((channels, FAST), F32)
        for direction in range(steering.shape[0]):
            residue = jnp.where(wanted == direction, steering[direction : direction + 1, :], residue)
        residue = jnp.where(counted > slot, residue, 0.0)
        for earlier in found:
            residue = residue - earlier * jnp.sum(earlier * residue, axis=-1, keepdims=True)
        found.append(residue / jnp.sqrt(jnp.sum(residue * residue, axis=-1, keepdims=True) + EPSILON))
    identity = (
        lax.broadcasted_iota(jnp.int32, (FAST, FAST), 0) == lax.broadcasted_iota(jnp.int32, (FAST, FAST), 1)
    ).astype(F32)
    for channel in range(channels):
        basis = jnp.concatenate([vector[channel : channel + 1, :] for vector in found], axis=0)
        keep = identity - lax.dot_general(
            basis, basis, (((0,), (0,)), ((), ())), precision=HIGHEST, preferred_element_type=F32
        )
        keep_h, keep_l = split(keep)
        below[channel] = beside(keep_h, keep_l, 0)
        aside[channel] = beside(keep_h, keep_l, 1)

    gram_ref[...] = jnp.zeros(gram_ref.shape, F32)
    lower = lax.broadcasted_iota(jnp.int32, (groups, FAST), 1) < frames

    def gather(pair, use):
        for which in range(2):
            part = landed.at[pl.ds((2 * pair + which) * groups, groups)]
            pltpu.make_async_copy(part, part, recv_sem.at[2 * pair + which]).wait()
            wide[which * 8 * groups : (which + 1) * 8 * groups, :] = part[...].astype(F32).reshape(8 * groups, FAST)
        for channel in range(channels):
            for half in range(2):
                first = wide[pl.ds(half * 4 + channel, groups, stride=8), :]
                second = wide[pl.ds(8 * groups + half * 4 + channel, groups, stride=8), :]
                sides[channel, pl.ds(half * FAST, groups, stride=2), :] = jnp.where(
                    lower, first, pltpu.roll(second, frames, 1)
                )
                sides[channel, pl.ds(half * FAST + 1, groups, stride=2), :] = jnp.where(
                    lower, pltpu.roll(first, frames, 1), second
                )
            side = sides[channel].astype(BF16)
            outer = dot_t(side, side)
            real = gram_ref[channel, :FAST] + (outer[:FAST, :FAST] + outer[FAST:, FAST:])
            imag = gram_ref[channel, FAST:] + (outer[FAST:, :FAST] - outer[:FAST, FAST:])
            use(channel, jnp.concatenate([real, imag], axis=0))

    def keep_sum(channel, gram):
        gram_ref[channel] = gram

    def early(pair, carry):
        gather(pair, keep_sum)
        return carry

    lax.fori_loop(0, nt // 2 - 1, early, 0)
    others = pl.ds(0, nt * groups - 1)
    pltpu.make_async_copy(pieces.at[others], pieces.at[others], send_sem).wait()

    @pl.when(shard < nt - 1)
    def _():
        for copy in carried:
            copy.wait_send()

    def project(channel, gram):
        gram_h, gram_l = split(gram)
        left = dot(jnp.concatenate([gram_h, gram_h, gram_l], axis=1), below[channel])
        left_h, left_l = split(jnp.concatenate([left[:FAST], left[FAST:]], axis=1))
        result = dot(aside[channel], jnp.concatenate([left_h, left_h, left_l], axis=0)) * (1.0 / (frames * nt))
        out_ref[channel, 0] = result[:, :FAST]
        out_ref[channel, 1] = result[:, FAST:]

    gather(nt // 2 - 1, project)


def covariance(now, taps, steering, chosen, counted):
    extents = (16, 4, 4, 2)
    near = [8]
    for d in range(7, 0, -1):
        near += [d, 16 - d]
    near.append(0)

    def kernel(*refs):
        covariance_kernel(extents, near, *refs)

    frames, rows, _ = now.shape
    tap_count, length = taps.shape
    channels = chosen.shape[0]
    w1_high, w1_low = first_stage_matrix()
    w1 = np.concatenate([w1_high, w1_low, w1_high], axis=1)
    w2_high, w2_low = second_stage_matrix()
    w2 = np.concatenate([w2_high, w2_low, w2_high], axis=1)
    table = twiddles()
    vmem = pl.BlockSpec(memory_space=pltpu.VMEM)
    hbm = pl.BlockSpec(memory_space=pltpu.HBM)
    dma = pltpu.SemaphoreType.DMA
    return pl.pallas_call(
        kernel,
        out_shape=jax.ShapeDtypeStruct((channels, 2, FAST, FAST), F32),
        in_specs=[hbm] * 8,
        out_specs=vmem,
        scratch_shapes=[
            pltpu.VMEM((frames + tap_count - 1, rows, FAST), BF16),
            pltpu.VMEM((frames + tap_count - 1, rows, FAST), F32),
            pltpu.VMEM((tap_count, length), F32),
            pltpu.VMEM((tap_count * rows, FAST), F32),
            pltpu.VMEM((8, rows, FAST), F32),
            pltpu.VMEM((8, rows, FAST), F32),
            pltpu.VMEM((SLOW + 2, 2 * frames, FAST), F32),
            pltpu.VMEM((512, FAST), F32),
            pltpu.VMEM((512, 8, FAST), BF16),
            pltpu.VMEM((512, 8, FAST), BF16),
            pltpu.VMEM((1024, FAST), F32),
            pltpu.VMEM((channels, 2 * FAST, FAST), F32),
            pltpu.VMEM((channels, 2 * FAST, FAST), F32),
            pltpu.VMEM((channels, 3 * FAST, FAST), BF16),
            pltpu.VMEM((channels, FAST, 3 * FAST), BF16),
            pltpu.VMEM(steering.shape, F32),
            pltpu.VMEM(chosen.shape, jnp.int32),
            pltpu.SMEM(counted.shape, jnp.int32),
            pltpu.VMEM(w1.shape, BF16),
            pltpu.VMEM(w2.shape, BF16),
            pltpu.VMEM(table.shape, F32),
            dma((frames // 16,)),
            dma((7,)),
            dma((2,)),
            dma((2,)),
            dma,
            dma((8,)),
            pltpu.SemaphoreType.REGULAR,
            pltpu.SemaphoreType.REGULAR((8,)),
        ],
        compiler_params=pltpu.CompilerParams(collective_id=0, has_side_effects=True, vmem_limit_bytes=40 << 20),
        cost_estimate=pl.CostEstimate(flops=10**9, bytes_accessed=4 << 20, transcendentals=0),
    )(
        *(
            pltpu.with_memory_space_constraint(value, pltpu.HBM)
            for value in (now, taps, jnp.asarray(w1), jnp.asarray(w2), jnp.asarray(table), steering, chosen, counted)
        )
    )


def per_device(samples, taps, steering, interferer_ids, ranks):
    antennas, width = samples.shape
    length = taps.shape[1]
    frames = width // length
    blocks = samples.reshape(antennas, frames * SLOW, FAST).transpose(1, 0, 2).reshape(frames, SLOW * antennas, FAST)
    return covariance(blocks, taps, steering, interferer_ids, ranks)


def solution(mesh):
    in_specs = (P("chan", "tm"), P(), P(), P(("chan", "tm"), None), P(("chan", "tm")))
    out_specs = P(("chan", "tm"), None, None, None)
    return jax.shard_map(per_device, mesh=mesh, in_specs=in_specs, out_specs=out_specs, check_vma=False)
```

```python
import jax
import jax.numpy as jnp
import numpy as np
from jax import lax
from jax.experimental import pallas as pl
from jax.experimental.pallas import tpu as pltpu
from jax.sharding import PartitionSpec as P

SLOW = 32
FAST = 128
EPSILON = 1e-06
F32 = jnp.float32
BF16 = jnp.bfloat16
HIGHEST = lax.Precision.HIGHEST


def split_constant(values):
    high = values.astype(np.float32).astype(jnp.bfloat16)
    low = (values - high.astype(np.float64)).astype(np.float32).astype(jnp.bfloat16)
    return high, low


def first_stage_matrix():
    p = np.arange(SLOW)
    rows = []
    for k1 in range(SLOW // 2 + 1):
        angle = 2.0 * np.pi * (k1 * p % SLOW) / SLOW
        rows.append(np.cos(angle))
        rows.append(-np.sin(angle) if k1 % (SLOW // 2) else np.zeros(SLOW))
    coefficients = np.stack(rows)
    full = np.einsum("kp,fg->kfgp", coefficients, np.eye(8)).reshape(len(rows) * 8, 8 * SLOW)
    return split_constant(full)


def second_stage_matrix():
    turns = np.outer(np.arange(64), np.arange(FAST)) % FAST
    angle = 2.0 * np.pi * turns / FAST
    real_rows = np.concatenate([np.cos(angle), np.sin(angle)], axis=1)
    imag_rows = np.concatenate([-np.sin(angle), np.cos(angle)], axis=1)
    return split_constant(np.concatenate([real_rows, imag_rows], axis=0))


def twiddles():
    angle = 2.0 * np.pi * np.outer(np.arange(SLOW), np.arange(FAST)) / (SLOW * FAST)
    sign = np.where(np.arange(SLOW) > SLOW // 2, -1.0, 1.0)[:, None]
    return np.stack([np.cos(angle), np.sin(angle), sign * np.cos(angle), sign * np.sin(angle)]).astype(np.float32)


def split(values):
    high = values.astype(BF16)
    return high, (values - high.astype(F32)).astype(BF16)


def beside(high, low, axis):
    return jnp.concatenate([high, low, high], axis=axis)


def dot(a, b):
    return lax.dot_general(a, b, (((1,), (0,)), ((), ())), preferred_element_type=F32)


def dot_t(a, b):
    return lax.dot_general(a, b, (((1,), (1,)), ((), ())), preferred_element_type=F32)


def covariance_kernel(extents, near, now_ref, taps_ref, w1_ref, w2_ref, table_ref, steering_ref, chosen_ref, counted_ref,
                      out_ref, arrived, window, taps, weights, early_part, late_part, y, spectrum, pieces, landed, wide, sides,
                      gram_ref, below, aside, steering, chosen, counted_scalar, w1, w2, table, in_sem, const_sem, halo_send, halo_recv, send_sem, recv_sem,
                      plane_sem, whole_sem):
    nz, nx, ny, nc = extents
    nt = ny * nc
    groups = nz * nx
    tap_count = taps_ref.shape[0]
    halo = tap_count - 1
    frames, rows, _ = now_ref.shape
    channels, slots = chosen_ref.shape
    group = lax.axis_index("chan")
    shard = lax.axis_index("tm")
    z, x = group // nx, lax.rem(group, nx)

    def along_z(d):
        return {"chan": lax.rem(z + d, nz) * nx + x}

    def along_x(d):
        return {"chan": z * nx + lax.rem(x + d, nx)}

    def along_t(d):
        return {"tm": lax.rem(shard + d, nt)}

    pairs = (
        (taps_ref, taps),
        (w1_ref, w1),
        (w2_ref, w2),
        (table_ref, table),
        (steering_ref, steering),
        (chosen_ref, chosen),
        (counted_ref, counted_scalar),
    )
    constants = [
        pltpu.make_async_copy(source, target, const_sem.at[i])
        for i, (source, target) in enumerate(pairs)
    ]
    inputs = [
        pltpu.make_async_copy(now_ref.at[pl.ds(i * 16, 16)], arrived.at[pl.ds(halo + i * 16, 16)], in_sem.at[i])
        for i in range(frames // 16)
    ]
    for copy in constants[:1] + inputs + constants[1:]:
        copy.start()

    barrier = pltpu.get_barrier_semaphore()
    for d in near[:-1]:
        pl.semaphore_signal(barrier, inc=1, device_id=along_z(d))
    for count, line in ((nt, along_t), (nx, along_x)):
        for d in range(1, count):
            pl.semaphore_signal(barrier, inc=1, device_id=line(d))

    @pl.when(shard == 0)
    def _():
        arrived[0:halo] = jnp.zeros((halo, rows, FAST), BF16)

    constants[0].wait()
    for p in range(SLOW):
        for t in range(0, tap_count, 8):
            tile = taps[t : t + 8, p * FAST : (p + 1) * FAST]
            for a in range(2):
                weights[pl.ds(t * rows + 2 * p + a, 8, stride=rows), :] = tile

    def widen(first, last):
        window[first:last] = arrived[first:last].astype(F32)

    def widen_group(g):
        if g % 2 == 0:
            inputs[g // 2].wait()
        widen(halo + g * 8, halo + g * 8 + 8)

    def filter_group(g, filtered, place):
        for r in range(0, rows, 8):
            tap = [weights[t * rows + r : t * rows + r + 8, :] for t in range(tap_count)]
            seen = [window[g * 8 + i, r : r + 8, :] for i in range(8 + halo)]
            for f in range(8):
                result = tap[0] * seen[f]
                for t in range(1, tap_count):
                    result = result + tap[t] * seen[f + t]
                filtered[place * 8 + f, r : r + 8, :] = result

    def turn_groups(order, filtered):
        columns_h, columns_l = [], []
        for place in range(len(order)):
            for a in range(2):
                parts = [split(filtered[place * 8 + f, pl.ds(a, SLOW, stride=2), :]) for f in range(8)]
                columns_h.append(jnp.concatenate([h for h, _ in parts], axis=0))
                columns_l.append(jnp.concatenate([l for _, l in parts], axis=0))
        xh = jnp.concatenate(columns_h, axis=1)
        xl = jnp.concatenate(columns_l, axis=1)
        turned = dot(w1[...], jnp.concatenate([xh, xh, xl], axis=0))
        for place, g in enumerate(order):
            for a in range(2):
                at = (2 * place + a) * FAST
                piece = turned[:, at : at + FAST].reshape(SLOW + 2, 8, FAST)
                y[:, a * frames + g * 8 : a * frames + g * 8 + 8, :] = piece

    for g in range(3):
        widen_group(g)
    filter_group(2, early_part, 0)
    constants[1].wait()
    widen_group(3)
    filter_group(3, early_part, 1)

    pl.semaphore_wait(barrier, nz + nx + nt - 3)
    near_halo = halo // 2
    carried = [
        pltpu.make_async_remote_copy(
            src_ref=now_ref.at[pl.ds(frames - halo + first, count)],
            dst_ref=arrived.at[pl.ds(first, count)],
            send_sem=halo_send.at[i],
            recv_sem=halo_recv.at[i],
            device_id=along_t(1),
        )
        for i, (first, count) in enumerate(((halo - near_halo, near_halo), (0, halo - near_halo)))
    ]

    @pl.when(shard < nt - 1)
    def _():
        for copy in carried:
            copy.start()

    for d in range(1, nx):
        pl.semaphore_signal(plane_sem, inc=1, device_id=along_x(d))

    for g in (4, 5):
        widen_group(g)
        filter_group(g, early_part, g - 2)
    turn_groups((2, 3, 4, 5), early_part)
    for g in (6, 7):
        widen_group(g)
        filter_group(g, late_part, g - 6)

    @pl.when(shard > 0)
    def _():
        carried[0].wait_recv()

    widen(halo - near_halo, halo)
    filter_group(1, late_part, 2)

    @pl.when(shard > 0)
    def _():
        carried[1].wait_recv()

    widen(0, halo - near_halo)
    filter_group(0, late_part, 3)
    turn_groups((6, 7, 1, 0), late_part)
    for copy in constants[2:]:
        copy.wait()

    def finish(i):
        to_shard = lax.rem(shard + i, nt)
        for sub in range(4):
            k1 = to_shard * 4 + sub
            j = jnp.minimum(k1, SLOW - k1)
            real, imag = y[2 * j], y[2 * j + 1]
            cos, sin, signed_cos, signed_sin = (table[n, pl.ds(k1, 1), :] for n in range(4))
            zr = real * cos + imag * signed_sin
            zi = imag * signed_cos - real * sin
            zh, zl = split(jnp.concatenate([zr, zi], axis=1))
            result = dot_t(w2[...], jnp.concatenate([zh, zh, zl], axis=1))
            for part in range(2):
                spectrum[pl.ds(part * 4 + sub, 64, stride=8), :] = result[part * 64 : (part + 1) * 64]
        base = pl.multiple_of(i * groups, groups)
        pieces[pl.ds(base, groups)] = spectrum[...].reshape(groups, 8, FAST).astype(BF16)

    def send(i, dz, dx):
        to_shard = lax.rem(shard + i, nt)
        to_group = lax.rem(z + dz, nz) * nx + lax.rem(x + dx, nx)
        pltpu.make_async_remote_copy(
            src_ref=pieces.at[i * groups + to_group],
            dst_ref=landed.at[i * groups + group],
            send_sem=send_sem,
            recv_sem=recv_sem.at[i],
            device_id={"chan": to_group, "tm": to_shard},
        ).start()

    def columns(i, first):
        def column(dx, carry):
            for dz in near:
                send(i, dz, dx)
            return carry

        lax.fori_loop(first, nx, column, 0)

    zero = jnp.int32(0)
    finish(zero)
    for dz in near[:-1]:
        send(zero, dz, 0)
    pltpu.make_async_copy(pieces.at[group], landed.at[group], recv_sem.at[0]).start()
    pl.semaphore_wait(plane_sem, nx - 1)
    for d in range(1, nt):
        pl.semaphore_signal(whole_sem.at[nt - d], inc=1, device_id=along_t(d))
    columns(zero, 1)

    def onward(i, carry):
        finish(i)
        pl.semaphore_wait(whole_sem.at[i], 1)
        columns(i, 0)
        return carry

    lax.fori_loop(1, nt, onward, 0)

    row = lax.broadcasted_iota(jnp.int32, (channels, FAST), 0)
    counted = jnp.zeros((channels, FAST), jnp.int32)
    for channel in range(channels):
        counted = jnp.where(row == channel, counted_scalar[channel], counted)
    found = []
    for slot in range(slots):
        wanted = chosen[:, slot : slot + 1]
        residue = jnp.zeros((channels, FAST), F32)
        for direction in range(steering.shape[0]):
            residue = jnp.where(wanted == direction, steering[direction : direction + 1, :], residue)
        residue = jnp.where(counted > slot, residue, 0.0)
        for earlier in found:
            residue = residue - earlier * jnp.sum(earlier * residue, axis=-1, keepdims=True)
        found.append(residue / jnp.sqrt(jnp.sum(residue * residue, axis=-1, keepdims=True) + EPSILON))
    identity = (
        lax.broadcasted_iota(jnp.int32, (FAST, FAST), 0) == lax.broadcasted_iota(jnp.int32, (FAST, FAST), 1)
    ).astype(F32)
    for channel in range(channels):
        basis = jnp.concatenate([vector[channel : channel + 1, :] for vector in found], axis=0)
        keep = identity - lax.dot_general(
            basis, basis, (((0,), (0,)), ((), ())), precision=HIGHEST, preferred_element_type=F32
        )
        keep_h, keep_l = split(keep)
        below[channel] = beside(keep_h, keep_l, 0)
        aside[channel] = beside(keep_h, keep_l, 1)

    gram_ref[...] = jnp.zeros(gram_ref.shape, F32)
    lower = lax.broadcasted_iota(jnp.int32, (groups, FAST), 1) < frames

    def gather(pair, use):
        for which in range(2):
            part = landed.at[pl.ds((2 * pair + which) * groups, groups)]
            pltpu.make_async_copy(part, part, recv_sem.at[2 * pair + which]).wait()
            wide[which * 8 * groups : (which + 1) * 8 * groups, :] = part[...].astype(F32).reshape(8 * groups, FAST)
        for channel in range(channels):
            for half in range(2):
                first = wide[pl.ds(half * 4 + channel, groups, stride=8), :]
                second = wide[pl.ds(8 * groups + half * 4 + channel, groups, stride=8), :]
                sides[channel, pl.ds(half * FAST, groups, stride=2), :] = jnp.where(
                    lower, first, pltpu.roll(second, frames, 1)
                )
                sides[channel, pl.ds(half * FAST + 1, groups, stride=2), :] = jnp.where(
                    lower, pltpu.roll(first, frames, 1), second
                )
            side = sides[channel].astype(BF16)
            outer = dot_t(side, side)
            real = gram_ref[channel, :FAST] + (outer[:FAST, :FAST] + outer[FAST:, FAST:])
            imag = gram_ref[channel, FAST:] + (outer[FAST:, :FAST] - outer[:FAST, FAST:])
            use(channel, jnp.concatenate([real, imag], axis=0))

    def keep_sum(channel, gram):
        gram_ref[channel] = gram

    def early(pair, carry):
        gather(pair, keep_sum)
        return carry

    lax.fori_loop(0, nt // 2 - 1, early, 0)
    others = pl.ds(0, nt * groups - 1)
    pltpu.make_async_copy(pieces.at[others], pieces.at[others], send_sem).wait()

    @pl.when(shard < nt - 1)
    def _():
        for copy in carried:
            copy.wait_send()

    def project(channel, gram):
        gram_h, gram_l = split(gram)
        left = dot(jnp.concatenate([gram_h, gram_h, gram_l], axis=1), below[channel])
        left_h, left_l = split(jnp.concatenate([left[:FAST], left[FAST:]], axis=1))
        result = dot(aside[channel], jnp.concatenate([left_h, left_h, left_l], axis=0)) * (1.0 / (frames * nt))
        out_ref[channel, 0] = result[:, :FAST]
        out_ref[channel, 1] = result[:, FAST:]

    gather(nt // 2 - 1, project)


def covariance(now, taps, steering, chosen, counted):
    extents = (16, 4, 4, 2)
    near = [8]
    for d in range(7, 0, -1):
        near += [d, 16 - d]
    near.append(0)

    def kernel(*refs):
        covariance_kernel(extents, near, *refs)

    frames, rows, _ = now.shape
    tap_count, length = taps.shape
    channels = chosen.shape[0]
    w1_high, w1_low = first_stage_matrix()
    w1 = np.concatenate([w1_high, w1_low, w1_high], axis=1)
    w2_high, w2_low = second_stage_matrix()
    w2 = np.concatenate([w2_high, w2_low, w2_high], axis=1)
    table = twiddles()
    vmem = pl.BlockSpec(memory_space=pltpu.VMEM)
    hbm = pl.BlockSpec(memory_space=pltpu.HBM)
    dma = pltpu.SemaphoreType.DMA
    return pl.pallas_call(
        kernel,
        out_shape=jax.ShapeDtypeStruct((channels, 2, FAST, FAST), F32),
        in_specs=[hbm] * 8,
        out_specs=vmem,
        scratch_shapes=[
            pltpu.VMEM((frames + tap_count - 1, rows, FAST), BF16),
            pltpu.VMEM((frames + tap_count - 1, rows, FAST), F32),
            pltpu.VMEM((tap_count, length), F32),
            pltpu.VMEM((tap_count * rows, FAST), F32),
            pltpu.VMEM((32, rows, FAST), F32),
            pltpu.VMEM((32, rows, FAST), F32),
            pltpu.VMEM((SLOW + 2, 2 * frames, FAST), F32),
            pltpu.VMEM((512, FAST), F32),
            pltpu.VMEM((512, 8, FAST), BF16),
            pltpu.VMEM((512, 8, FAST), BF16),
            pltpu.VMEM((1024, FAST), F32),
            pltpu.VMEM((channels, 2 * FAST, FAST), F32),
            pltpu.VMEM((channels, 2 * FAST, FAST), F32),
            pltpu.VMEM((channels, 3 * FAST, FAST), BF16),
            pltpu.VMEM((channels, FAST, 3 * FAST), BF16),
            pltpu.VMEM(steering.shape, F32),
            pltpu.VMEM(chosen.shape, jnp.int32),
            pltpu.SMEM(counted.shape, jnp.int32),
            pltpu.VMEM(w1.shape, BF16),
            pltpu.VMEM(w2.shape, BF16),
            pltpu.VMEM(table.shape, F32),
            dma((frames // 16,)),
            dma((7,)),
            dma((2,)),
            dma((2,)),
            dma,
            dma((8,)),
            pltpu.SemaphoreType.REGULAR,
            pltpu.SemaphoreType.REGULAR((8,)),
        ],
        compiler_params=pltpu.CompilerParams(collective_id=0, has_side_effects=True, vmem_limit_bytes=40 << 20),
        cost_estimate=pl.CostEstimate(flops=10**9, bytes_accessed=4 << 20, transcendentals=0),
    )(
        *(
            pltpu.with_memory_space_constraint(value, pltpu.HBM)
            for value in (now, taps, jnp.asarray(w1), jnp.asarray(w2), jnp.asarray(table), steering, chosen, counted)
        )
    )


def per_device(samples, taps, steering, interferer_ids, ranks):
    antennas, width = samples.shape
    length = taps.shape[1]
    frames = width // length
    blocks = samples.reshape(antennas, frames * SLOW, FAST).transpose(1, 0, 2).reshape(frames, SLOW * antennas, FAST)
    return covariance(blocks, taps, steering, interferer_ids, ranks)


def solution(mesh):
    in_specs = (P("chan", "tm"), P(), P(), P(("chan", "tm"), None), P(("chan", "tm")))
    out_specs = P(("chan", "tm"), None, None, None)
    return jax.shard_map(per_device, mesh=mesh, in_specs=in_specs, out_specs=out_specs, check_vma=False)
```

```python
import jax
import jax.numpy as jnp
import numpy as np
from jax import lax
from jax.experimental import pallas as pl
from jax.experimental.pallas import tpu as pltpu
from jax.sharding import PartitionSpec as P

SLOW = 32
FAST = 128
EPSILON = 1e-06
F32 = jnp.float32
BF16 = jnp.bfloat16
HIGHEST = lax.Precision.HIGHEST


def split_constant(values):
    high = values.astype(np.float32).astype(jnp.bfloat16)
    low = (values - high.astype(np.float64)).astype(np.float32).astype(jnp.bfloat16)
    return high, low


def first_stage_matrix():
    p = np.arange(SLOW)
    rows = []
    for k1 in range(SLOW // 2 + 1):
        angle = 2.0 * np.pi * (k1 * p % SLOW) / SLOW
        rows.append(np.cos(angle))
        rows.append(-np.sin(angle) if k1 % (SLOW // 2) else np.zeros(SLOW))
    coefficients = np.stack(rows)
    full = np.einsum("kp,fg->kfgp", coefficients, np.eye(8)).reshape(len(rows) * 8, 8 * SLOW)
    return split_constant(full)


def second_stage_matrix():
    turns = np.outer(np.arange(64), np.arange(FAST)) % FAST
    angle = 2.0 * np.pi * turns / FAST
    real_rows = np.concatenate([np.cos(angle), np.sin(angle)], axis=1)
    imag_rows = np.concatenate([-np.sin(angle), np.cos(angle)], axis=1)
    return split_constant(np.concatenate([real_rows, imag_rows], axis=0))


def twiddles():
    angle = 2.0 * np.pi * np.outer(np.arange(SLOW), np.arange(FAST)) / (SLOW * FAST)
    sign = np.where(np.arange(SLOW) > SLOW // 2, -1.0, 1.0)[:, None]
    return np.stack([np.cos(angle), np.sin(angle), sign * np.cos(angle), sign * np.sin(angle)]).astype(np.float32)


def split(values):
    high = values.astype(BF16)
    return high, (values - high.astype(F32)).astype(BF16)


def beside(high, low, axis):
    return jnp.concatenate([high, low, high], axis=axis)


def dot(a, b):
    return lax.dot_general(a, b, (((1,), (0,)), ((), ())), preferred_element_type=F32)


def dot_t(a, b):
    return lax.dot_general(a, b, (((1,), (1,)), ((), ())), preferred_element_type=F32)


def covariance_kernel(extents, near, now_ref, taps_ref, w1_ref, w2_ref, table_ref, steering_ref, chosen_ref, counted_ref,
                      out_ref, arrived, window, taps, weights, early_part, late_part, y, spectrum, pieces, landed, wide, sides,
                      gram_ref, below, aside, steering, chosen, counted_scalar, w1, w2, table, in_sem, const_sem, halo_send, halo_recv, send_sem, recv_sem,
                      plane_sem, whole_sem):
    nz, nx, ny, nc = extents
    nt = ny * nc
    groups = nz * nx
    tap_count = taps_ref.shape[0]
    halo = tap_count - 1
    frames, rows, _ = now_ref.shape
    channels, slots = chosen_ref.shape
    group = lax.axis_index("chan")
    shard = lax.axis_index("tm")
    z, x = group // nx, lax.rem(group, nx)

    def along_z(d):
        return {"chan": lax.rem(z + d, nz) * nx + x}

    def along_x(d):
        return {"chan": z * nx + lax.rem(x + d, nx)}

    def along_t(d):
        return {"tm": lax.rem(shard + d, nt)}

    pairs = (
        (taps_ref, taps),
        (w1_ref, w1),
        (w2_ref, w2),
        (table_ref, table),
        (steering_ref, steering),
        (chosen_ref, chosen),
        (counted_ref, counted_scalar),
    )
    constants = [
        pltpu.make_async_copy(source, target, const_sem.at[i])
        for i, (source, target) in enumerate(pairs)
    ]
    inputs = [
        pltpu.make_async_copy(now_ref.at[pl.ds(i * 16, 16)], arrived.at[pl.ds(halo + i * 16, 16)], in_sem.at[i])
        for i in range(frames // 16)
    ]
    for copy in constants[:1] + inputs + constants[1:]:
        copy.start()

    barrier = pltpu.get_barrier_semaphore()
    for d in near[:-1]:
        pl.semaphore_signal(barrier, inc=1, device_id=along_z(d))
    for count, line in ((nt, along_t), (nx, along_x)):
        for d in range(1, count):
            pl.semaphore_signal(barrier, inc=1, device_id=line(d))

    @pl.when(shard == 0)
    def _():
        arrived[0:halo] = jnp.zeros((halo, rows, FAST), BF16)

    constants[0].wait()
    for p in range(SLOW):
        for t in range(0, tap_count, 8):
            tile = taps[t : t + 8, p * FAST : (p + 1) * FAST]
            for a in range(2):
                weights[pl.ds(t * rows + 2 * p + a, 8, stride=rows), :] = tile

    def widen(first, last):
        window[first:last] = arrived[first:last].astype(F32)

    def widen_group(g):
        if g % 2 == 0:
            inputs[g // 2].wait()
        widen(halo + g * 8, halo + g * 8 + 8)

    def filter_group(g, filtered, place):
        for r in range(0, rows, 8):
            tap = [weights[t * rows + r : t * rows + r + 8, :] for t in range(tap_count)]
            seen = [window[g * 8 + i, r : r + 8, :] for i in range(8 + halo)]
            for f in range(8):
                result = tap[0] * seen[f]
                for t in range(1, tap_count):
                    result = result + tap[t] * seen[f + t]
                filtered[place * 8 + f, r : r + 8, :] = result

    def turn_groups(order, filtered):
        columns_h, columns_l = [], []
        for place in range(len(order)):
            for a in range(2):
                parts = [split(filtered[place * 8 + f, pl.ds(a, SLOW, stride=2), :]) for f in range(8)]
                columns_h.append(jnp.concatenate([h for h, _ in parts], axis=0))
                columns_l.append(jnp.concatenate([l for _, l in parts], axis=0))
        xh = jnp.concatenate(columns_h, axis=1)
        xl = jnp.concatenate(columns_l, axis=1)
        turned = dot(w1[...], jnp.concatenate([xh, xh, xl], axis=0))
        for place, g in enumerate(order):
            for a in range(2):
                at = (2 * place + a) * FAST
                piece = turned[:, at : at + FAST].reshape(SLOW + 2, 8, FAST)
                y[:, a * frames + g * 8 : a * frames + g * 8 + 8, :] = piece

    for g in range(3):
        widen_group(g)
    filter_group(2, early_part, 0)
    constants[1].wait()
    widen_group(3)
    filter_group(3, early_part, 1)

    pl.semaphore_wait(barrier, nz + nx + nt - 3)
    near_halo = halo // 2
    carried = [
        pltpu.make_async_remote_copy(
            src_ref=now_ref.at[pl.ds(frames - halo + first, count)],
            dst_ref=arrived.at[pl.ds(first, count)],
            send_sem=halo_send.at[i],
            recv_sem=halo_recv.at[i],
            device_id=along_t(1),
        )
        for i, (first, count) in enumerate(((halo - near_halo, near_halo), (0, halo - near_halo)))
    ]

    @pl.when(shard < nt - 1)
    def _():
        for copy in carried:
            copy.start()

    for d in range(1, nx):
        pl.semaphore_signal(plane_sem, inc=1, device_id=along_x(d))

    for g in (4, 5):
        widen_group(g)
        filter_group(g, early_part, g - 2)
    turn_groups((2, 3, 4, 5), early_part)
    for g in (6, 7):
        widen_group(g)
        filter_group(g, late_part, g - 6)
    turn_groups((6, 7), late_part)

    @pl.when(shard > 0)
    def _():
        carried[0].wait_recv()

    widen(halo - near_halo, halo)
    filter_group(1, early_part, 0)

    @pl.when(shard > 0)
    def _():
        carried[1].wait_recv()

    widen(0, halo - near_halo)
    filter_group(0, early_part, 1)
    turn_groups((1, 0), early_part)
    for copy in constants[2:]:
        copy.wait()

    def finish(i):
        to_shard = lax.rem(shard + i, nt)
        for sub in range(4):
            k1 = to_shard * 4 + sub
            j = jnp.minimum(k1, SLOW - k1)
            real, imag = y[2 * j], y[2 * j + 1]
            cos, sin, signed_cos, signed_sin = (table[n, pl.ds(k1, 1), :] for n in range(4))
            zr = real * cos + imag * signed_sin
            zi = imag * signed_cos - real * sin
            zh, zl = split(jnp.concatenate([zr, zi], axis=1))
            result = dot_t(w2[...], jnp.concatenate([zh, zh, zl], axis=1))
            for part in range(2):
                spectrum[pl.ds(part * 4 + sub, 64, stride=8), :] = result[part * 64 : (part + 1) * 64]
        base = pl.multiple_of(i * groups, groups)
        pieces[pl.ds(base, groups)] = spectrum[...].reshape(groups, 8, FAST).astype(BF16)

    def send(i, dz, dx):
        to_shard = lax.rem(shard + i, nt)
        to_group = lax.rem(z + dz, nz) * nx + lax.rem(x + dx, nx)
        pltpu.make_async_remote_copy(
            src_ref=pieces.at[i * groups + to_group],
            dst_ref=landed.at[i * groups + group],
            send_sem=send_sem,
            recv_sem=recv_sem.at[i],
            device_id={"chan": to_group, "tm": to_shard},
        ).start()

    def columns(i, first):
        def column(dx, carry):
            for dz in near:
                send(i, dz, dx)
            return carry

        lax.fori_loop(first, nx, column, 0)

    zero = jnp.int32(0)
    finish(zero)
    for dz in near[:-1]:
        send(zero, dz, 0)
    pltpu.make_async_copy(pieces.at[group], landed.at[group], recv_sem.at[0]).start()
    pl.semaphore_wait(plane_sem, nx - 1)
    for d in range(1, nt):
        pl.semaphore_signal(whole_sem.at[nt - d], inc=1, device_id=along_t(d))
    columns(zero, 1)

    def onward(i, carry):
        finish(i)
        pl.semaphore_wait(whole_sem.at[i], 1)
        columns(i, 0)
        return carry

    lax.fori_loop(1, nt, onward, 0)

    row = lax.broadcasted_iota(jnp.int32, (channels, FAST), 0)
    counted = jnp.zeros((channels, FAST), jnp.int32)
    for channel in range(channels):
        counted = jnp.where(row == channel, counted_scalar[channel], counted)
    found = []
    for slot in range(slots):
        wanted = chosen[:, slot : slot + 1]
        residue = jnp.zeros((channels, FAST), F32)
        for direction in range(steering.shape[0]):
            residue = jnp.where(wanted == direction, steering[direction : direction + 1, :], residue)
        residue = jnp.where(counted > slot, residue, 0.0)
        for earlier in found:
            residue = residue - earlier * jnp.sum(earlier * residue, axis=-1, keepdims=True)
        found.append(residue / jnp.sqrt(jnp.sum(residue * residue, axis=-1, keepdims=True) + EPSILON))
    identity = (
        lax.broadcasted_iota(jnp.int32, (FAST, FAST), 0) == lax.broadcasted_iota(jnp.int32, (FAST, FAST), 1)
    ).astype(F32)
    for channel in range(channels):
        basis = jnp.concatenate([vector[channel : channel + 1, :] for vector in found], axis=0)
        keep = identity - lax.dot_general(
            basis, basis, (((0,), (0,)), ((), ())), precision=HIGHEST, preferred_element_type=F32
        )
        keep_h, keep_l = split(keep)
        below[channel] = beside(keep_h, keep_l, 0)
        aside[channel] = beside(keep_h, keep_l, 1)

    gram_ref[...] = jnp.zeros(gram_ref.shape, F32)
    lower = lax.broadcasted_iota(jnp.int32, (groups, FAST), 1) < frames

    def gather(pair, use):
        for which in range(2):
            part = landed.at[pl.ds((2 * pair + which) * groups, groups)]
            pltpu.make_async_copy(part, part, recv_sem.at[2 * pair + which]).wait()
            wide[which * 8 * groups : (which + 1) * 8 * groups, :] = part[...].astype(F32).reshape(8 * groups, FAST)
        for channel in range(channels):
            for half in range(2):
                first = wide[pl.ds(half * 4 + channel, groups, stride=8), :]
                second = wide[pl.ds(8 * groups + half * 4 + channel, groups, stride=8), :]
                sides[channel, pl.ds(half * FAST, groups, stride=2), :] = jnp.where(
                    lower, first, pltpu.roll(second, frames, 1)
                )
                sides[channel, pl.ds(half * FAST + 1, groups, stride=2), :] = jnp.where(
                    lower, pltpu.roll(first, frames, 1), second
                )
            side = sides[channel].astype(BF16)
            outer = dot_t(side, side)
            real = gram_ref[channel, :FAST] + (outer[:FAST, :FAST] + outer[FAST:, FAST:])
            imag = gram_ref[channel, FAST:] + (outer[FAST:, :FAST] - outer[:FAST, FAST:])
            use(channel, jnp.concatenate([real, imag], axis=0))

    def keep_sum(channel, gram):
        gram_ref[channel] = gram

    def early(pair, carry):
        gather(pair, keep_sum)
        return carry

    lax.fori_loop(0, nt // 2 - 1, early, 0)
    others = pl.ds(0, nt * groups - 1)
    pltpu.make_async_copy(pieces.at[others], pieces.at[others], send_sem).wait()

    @pl.when(shard < nt - 1)
    def _():
        for copy in carried:
            copy.wait_send()

    def project(channel, gram):
        gram_h, gram_l = split(gram)
        left = dot(jnp.concatenate([gram_h, gram_h, gram_l], axis=1), below[channel])
        left_h, left_l = split(jnp.concatenate([left[:FAST], left[FAST:]], axis=1))
        result = dot(aside[channel], jnp.concatenate([left_h, left_h, left_l], axis=0)) * (1.0 / (frames * nt))
        out_ref[channel, 0] = result[:, :FAST]
        out_ref[channel, 1] = result[:, FAST:]

    gather(nt // 2 - 1, project)


def covariance(now, taps, steering, chosen, counted):
    extents = (16, 4, 4, 2)
    near = [8]
    for d in range(7, 0, -1):
        near += [d, 16 - d]
    near.append(0)

    def kernel(*refs):
        covariance_kernel(extents, near, *refs)

    frames, rows, _ = now.shape
    tap_count, length = taps.shape
    channels = chosen.shape[0]
    w1_high, w1_low = first_stage_matrix()
    w1 = np.concatenate([w1_high, w1_low, w1_high], axis=1)
    w2_high, w2_low = second_stage_matrix()
    w2 = np.concatenate([w2_high, w2_low, w2_high], axis=1)
    table = twiddles()
    vmem = pl.BlockSpec(memory_space=pltpu.VMEM)
    hbm = pl.BlockSpec(memory_space=pltpu.HBM)
    dma = pltpu.SemaphoreType.DMA
    return pl.pallas_call(
        kernel,
        out_shape=jax.ShapeDtypeStruct((channels, 2, FAST, FAST), F32),
        in_specs=[hbm] * 8,
        out_specs=vmem,
        scratch_shapes=[
            pltpu.VMEM((frames + tap_count - 1, rows, FAST), BF16),
            pltpu.VMEM((frames + tap_count - 1, rows, FAST), F32),
            pltpu.VMEM((tap_count, length), F32),
            pltpu.VMEM((tap_count * rows, FAST), F32),
            pltpu.VMEM((32, rows, FAST), F32),
            pltpu.VMEM((16, rows, FAST), F32),
            pltpu.VMEM((SLOW + 2, 2 * frames, FAST), F32),
            pltpu.VMEM((512, FAST), F32),
            pltpu.VMEM((512, 8, FAST), BF16),
            pltpu.VMEM((512, 8, FAST), BF16),
            pltpu.VMEM((1024, FAST), F32),
            pltpu.VMEM((channels, 2 * FAST, FAST), F32),
            pltpu.VMEM((channels, 2 * FAST, FAST), F32),
            pltpu.VMEM((channels, 3 * FAST, FAST), BF16),
            pltpu.VMEM((channels, FAST, 3 * FAST), BF16),
            pltpu.VMEM(steering.shape, F32),
            pltpu.VMEM(chosen.shape, jnp.int32),
            pltpu.SMEM(counted.shape, jnp.int32),
            pltpu.VMEM(w1.shape, BF16),
            pltpu.VMEM(w2.shape, BF16),
            pltpu.VMEM(table.shape, F32),
            dma((frames // 16,)),
            dma((7,)),
            dma((2,)),
            dma((2,)),
            dma,
            dma((8,)),
            pltpu.SemaphoreType.REGULAR,
            pltpu.SemaphoreType.REGULAR((8,)),
        ],
        compiler_params=pltpu.CompilerParams(collective_id=0, has_side_effects=True, vmem_limit_bytes=40 << 20),
        cost_estimate=pl.CostEstimate(flops=10**9, bytes_accessed=4 << 20, transcendentals=0),
    )(
        *(
            pltpu.with_memory_space_constraint(value, pltpu.HBM)
            for value in (now, taps, jnp.asarray(w1), jnp.asarray(w2), jnp.asarray(table), steering, chosen, counted)
        )
    )


def per_device(samples, taps, steering, interferer_ids, ranks):
    antennas, width = samples.shape
    length = taps.shape[1]
    frames = width // length
    blocks = samples.reshape(antennas, frames * SLOW, FAST).transpose(1, 0, 2).reshape(frames, SLOW * antennas, FAST)
    return covariance(blocks, taps, steering, interferer_ids, ranks)


def solution(mesh):
    in_specs = (P("chan", "tm"), P(), P(), P(("chan", "tm"), None), P(("chan", "tm")))
    out_specs = P(("chan", "tm"), None, None, None)
    return jax.shard_map(per_device, mesh=mesh, in_specs=in_specs, out_specs=out_specs, check_vma=False)
```
